512 devices in a mesh: ctx: 64 (over z, x), head: 8 (over y, core).
Axes of the slice: x: 4, y: 4, z: 16, core: 2. Of those that a mesh axis runs over, the one named last changes fastest.
Arguments:
- queries: bfloat16 [16384, 4096], P('ctx', 'head'), may hold values from -6 to 6
- keys: bfloat16 [16384, 4096], P('ctx', 'head'), may hold values from -6 to 6
- values: bfloat16 [16384, 4096], P('ctx', 'head'), may hold values from -6 to 6
- out_grad: bfloat16 [16384, 4096], P('ctx', 'head'), may hold values from -48 to 48
- outputs: bfloat16 [16384, 4096], P('ctx', 'head'), may hold values from -1.5 to 1.5
- log_norms: float32 [16384, 32], P('ctx', 'head'), may hold values from 4 to 7
- selected: int32 [128, 32, 3], P('ctx', 'head'), may hold values from -1 to 125, as said below
Outputs:
- grad_queries: bfloat16 [16384, 4096], P(('ctx', 'head'))
- grad_keys: bfloat16 [16384, 4096], P('ctx', 'head')
- grad_values: bfloat16 [16384, 4096], P('ctx', 'head')
The draws below stay inside these ranges and needn't reach their ends.
Inputs may be any that keep to these rules, and one draw needn't show every extreme that they name: `selected`: -1 marks no block; every other entry is a block held by a lower index of ctx than the query block's own, and the entries other than -1 of one query block and head differ. Among all entries of one index of ctx and one group of 4 heads, at most 2 name blocks held by any one other index of ctx; blocks may repeat across query blocks and heads.
All inputs are finite; a program needn't handle non-finite values.
Results may differ from the reference program's by a relative error of at most 0.0057.
Values may be sent and summed in bfloat16 or wider, within the bound.
No kernel may reach another device: no remote copies, remote signals or barrier semaphores. Data moves between devices by JAX's collectives and lax.ppermute only.
A program may use at most 64 MiB of HBM per device.

```python
import jax
import jax.numpy as jnp
from jax import lax

DH = 128
HEADS_DEV = 4
TOPK = 3
PER_PEER = 2
BLK_DEV = 2
HEADS = 32
BLOCK_COUNT = 128
TOKENS = 16384
N_CTX = 64
N_HEAD = 8


def choose_blocks(seed_key, device_position, block_demand, busiest_device):
    slot_count = BLK_DEV * HEADS_DEV * TOPK
    block_numbers = jnp.arange(BLOCK_COUNT, dtype=jnp.int32)
    owning_devices = block_numbers // BLK_DEV
    device_ids = jnp.arange(N_CTX, dtype=jnp.int32)
    random_jitter = jax.random.randint(seed_key, (slot_count, BLOCK_COUNT), 0, 1 << 15, dtype=jnp.int32)
    extra_reward = jnp.where(owning_devices == busiest_device, 1 << 19, 0).astype(jnp.int32)
    block_scores = (random_jitter * block_demand[None, :] + extra_reward[None, :]) * BLOCK_COUNT + block_numbers[None, :]
    earlier = block_numbers < device_position * BLK_DEV

    def step(carry, inputs):
        counts, taken = carry
        row, index = inputs
        taken = jnp.where(index % TOPK == 0, jnp.zeros_like(taken), taken)
        valid = earlier & (taken == 0) & (counts[owning_devices] < PER_PEER)
        masked = jnp.where(valid, row, -1)
        best = jnp.argmax(masked).astype(jnp.int32)
        found = jnp.any(valid)
        choice_made = jnp.where(found, best, -1).astype(jnp.int32)
        counts = counts + jnp.where(found & (device_ids == best // BLK_DEV), 1, 0).astype(jnp.int32)
        taken = taken + jnp.where(found & (block_numbers == best), 1, 0).astype(jnp.int32)
        return ((counts, taken), choice_made)
    start = (jnp.zeros((N_CTX,), jnp.int32), jnp.zeros((BLOCK_COUNT,), jnp.int32))
    ignored, picks = lax.scan(step, start, (block_scores, jnp.arange(slot_count, dtype=jnp.int32)))
    return picks


def draw_selected(key, part):
    popular_key, base_key = jax.random.split(jax.random.fold_in(key, 17), 2)
    block_demand = jax.random.randint(popular_key, (BLOCK_COUNT,), 1, 9, dtype=jnp.int32)
    busiest_device = jnp.zeros((), jnp.int32)

    def single_draw(position):
        return choose_blocks(jax.random.fold_in(base_key, position), position // N_HEAD, block_demand, busiest_device)
    flat = jax.vmap(single_draw)(jnp.arange(N_CTX * N_HEAD, dtype=jnp.int32))
    grid = flat.reshape(N_CTX, N_HEAD, BLK_DEV, HEADS_DEV, TOPK)
    grid = jnp.transpose(grid, (0, 2, 1, 3, 4))
    return grid.reshape(BLOCK_COUNT, HEADS, TOPK)


def block_scale(key, shape, shards, low, top_value):
    level = 1.0
    for axis_at, shards_of in shards:
        heights = jax.random.uniform(jax.random.fold_in(jax.random.fold_in(key, 6), axis_at), (shards_of,), jnp.float32, low / len(shards), top_value / len(shards))
        level = level * jnp.repeat(jnp.exp(heights), shape[axis_at] // shards_of).reshape((-1,) + (1,) * (len(shape) - 1 - axis_at))
    return level


def gaussian(rng, extent, spread, reach, shards=(), kind=jnp.bfloat16):
    array = spread * jax.random.normal(rng, extent, jnp.float32)
    if shards:
        array = array * block_scale(rng, extent, shards, -0.22, 0.18)
    return jnp.clip(array, -reach, reach).astype(kind)


def setup_inputs(seed: int = 0) -> dict:
    key_of = jax.random.split(jax.random.key(seed), 8)
    queries = gaussian(key_of[0], (TOKENS, HEADS * DH), 1.0, 6.0, ((0, 64), (1, 8)))
    keys = gaussian(key_of[1], (TOKENS, HEADS * DH), 1.0, 6.0, ((0, 64), (1, 8)))
    values = gaussian(key_of[2], (TOKENS, HEADS * DH), 1.0, 6.0, ((0, 64), (1, 8)))
    out_grad = gaussian(key_of[3], (TOKENS, HEADS * DH), 8.0, 48.0, ((0, 64), (1, 8)))
    outputs = gaussian(key_of[4], (TOKENS, HEADS * DH), 0.25, 1.5, ((0, 64), (1, 8)))
    log_norms = jnp.clip(4.0 + 3.0 * jax.random.uniform(key_of[5], (TOKENS, HEADS), jnp.float32) ** block_scale(key_of[5], (TOKENS, HEADS), ((0, 64), (1, 8)), -0.2, 0.2), 4.0, 7.0)
    selected = draw_selected(jax.random.fold_in(key_of[7], 71), 0)
    return dict(queries=queries, keys=keys, values=values, out_grad=out_grad, outputs=outputs, log_norms=log_norms, selected=selected)


def settle(terms):
    own = terms[:, :1]
    rest = lax.optimization_barrier(terms[:, 1:].astype(jnp.bfloat16)).astype(jnp.float32)
    return jnp.concatenate([own, rest], axis=1)


def head_grads(queries, keys, values, out_grad, outputs, log_norms, selected, column):
    tokens = queries.shape[0]
    heads = log_norms.shape[1]
    head_dim = queries.shape[1] // heads
    blocks = selected.shape[0]
    top_count = selected.shape[2]
    block_len = tokens // blocks
    factor = head_dim ** -0.5
    start = column * head_dim

    def pick(matrix):
        piece = lax.dynamic_slice_in_dim(matrix, start, head_dim, 1)
        return piece.astype(jnp.float32).reshape(blocks, block_len, head_dim)

    query_rows = pick(queries)
    key_rows = pick(keys)
    value_rows = pick(values)
    grad_rows = pick(out_grad)
    output_rows = pick(outputs)
    norms = lax.dynamic_index_in_dim(log_norms, column, 1, keepdims=False).reshape(blocks, block_len)
    deltas = jnp.sum(grad_rows * output_rows, axis=2)
    chosen = lax.dynamic_index_in_dim(selected, column, 1, keepdims=False)
    listed = jnp.concatenate([jnp.arange(blocks, dtype=jnp.int32)[:, None], chosen.astype(jnp.int32)], axis=1)
    alive = listed >= 0
    safe = jnp.where(alive, listed, 0).astype(jnp.int32)
    slots = top_count + 1
    key_width = slots * block_len
    key_sel = key_rows[safe].reshape(blocks, key_width, head_dim)
    value_sel = value_rows[safe].reshape(blocks, key_width, head_dim)
    position = jnp.arange(block_len)
    lower = position[:, None] >= position[None, :]
    slot_rule = jnp.concatenate([lower[None], jnp.ones((top_count, block_len, block_len), dtype=bool)], axis=0)
    allowed = slot_rule[None] & alive[:, :, None, None]
    allowed = jnp.transpose(allowed, (0, 2, 1, 3)).reshape(blocks, block_len, key_width)
    block_scores = jnp.einsum("nsd,nkd->nsk", query_rows, key_sel) * factor
    weights = jnp.where(allowed, jnp.exp(block_scores - norms[:, :, None]), 0.0)
    dweights = jnp.einsum("nsd,nkd->nsk", grad_rows, value_sel)
    dscores = weights * (dweights - deltas[:, :, None])
    weights_b = lax.optimization_barrier(weights.astype(jnp.bfloat16)).astype(jnp.float32)
    dscores_b = lax.optimization_barrier(dscores.astype(jnp.bfloat16)).astype(jnp.float32)
    dscore_four = dscores_b.reshape(blocks, block_len, slots, block_len)
    weight_four = weights_b.reshape(blocks, block_len, slots, block_len)
    key_four = key_sel.reshape(blocks, slots, block_len, head_dim)
    query_terms = jnp.einsum("nsjk,njkd->njsd", dscore_four, key_four) * factor
    key_terms = jnp.einsum("nsjk,nsd->njkd", dscore_four, query_rows) * factor
    value_terms = jnp.einsum("nsjk,nsd->njkd", weight_four, grad_rows)
    live_weight = alive.astype(jnp.float32)[:, :, None, None]
    grad_q = jnp.sum(settle(query_terms) * live_weight, axis=1)
    part_k = settle(key_terms) * live_weight
    part_v = settle(value_terms) * live_weight
    flat_index = safe.reshape(-1)
    grad_k = jnp.zeros((blocks, block_len, head_dim), jnp.float32).at[flat_index].add(part_k.reshape(-1, block_len, head_dim))
    grad_v = jnp.zeros((blocks, block_len, head_dim), jnp.float32).at[flat_index].add(part_v.reshape(-1, block_len, head_dim))
    return grad_q, grad_k, grad_v


def reference(queries, keys, values, out_grad, outputs, log_norms, selected):
    tokens, full_width = queries.shape
    heads = log_norms.shape[1]
    head_dim = full_width // heads

    def per_head(column):
        return head_grads(queries, keys, values, out_grad, outputs, log_norms, selected, column)

    grad_q, grad_k, grad_v = lax.map(per_head, jnp.arange(heads, dtype=jnp.int32))

    def merge_heads(stack):
        stack = stack.reshape(heads, tokens, head_dim)
        return jnp.transpose(stack, (1, 0, 2)).reshape(tokens, full_width).astype(jnp.bfloat16)

    return merge_heads(grad_q), merge_heads(grad_k), merge_heads(grad_v)
```

```python
import functools

import jax
import jax.numpy as jnp
from jax import lax
from jax.experimental import pallas as pl
from jax.experimental.pallas import tpu as pltpu
from jax.sharding import Mesh
from jax.sharding import PartitionSpec as P

X_SIZE = 4
BLOCK = 128
STAT_ROWS = 16
PER_PEER = 2
UNROLL = 2
F32 = jnp.float32
BF16 = jnp.bfloat16


def mm(left, right, left_dim, right_dim):
    return lax.dot_general(
        left, right, (((left_dim,), (right_dim,)), ((), ())), preferred_element_type=F32
    )


def three_parts(value):
    high = value.astype(BF16)
    rest = value - high.astype(F32)
    middle = rest.astype(BF16)
    low = (rest - middle.astype(F32)).astype(BF16)
    return high, middle, low


def pack_kernel(blocks, heads, q_ref, g_ref, o_ref, n_ref, out_ref):
    rows = blocks * BLOCK
    out_ref[0:rows, :] = q_ref[...]
    out_ref[rows : 2 * rows, :] = g_ref[...]
    for h in range(heads):
        cols = slice(h * BLOCK, (h + 1) * BLOCK)
        lines = []
        for b in range(blocks):
            at = slice(b * BLOCK, (b + 1) * BLOCK)
            product = g_ref[at, cols].astype(F32) * o_ref[at, cols].astype(F32)
            delta = jnp.sum(product.T, axis=0, keepdims=True)
            norm = jnp.broadcast_to(n_ref[at, h : h + 1], (BLOCK, BLOCK)).T[0:1]
            lines += list(three_parts(norm)) + list(three_parts(delta))
        lines = [line.astype(F32) for line in lines]
        pad = jnp.zeros((STAT_ROWS - len(lines), BLOCK), F32)
        out_ref[2 * rows :, cols] = jnp.concatenate(lines + [pad], axis=0).astype(BF16)


def stat_lines(tile, b):
    tile = tile.astype(F32)

    def line(at):
        return (tile[at : at + 1] + tile[at + 1 : at + 2]) + tile[at + 2 : at + 3]

    if isinstance(b, int):
        return line(6 * b), line(6 * b + 3)
    first = b == 0
    return jnp.where(first, line(0), line(6)), jnp.where(first, line(3), line(9))


def pair_terms(q, g, k, v, norm, delta, factor, keep):
    scores = mm(k, q, 1, 1) * factor
    weights = jnp.where(keep, jnp.exp(scores - norm), 0.0)
    dscores = weights * (mm(v, g, 1, 1) - delta)
    weights_b = weights.astype(BF16)
    dscores_b = dscores.astype(BF16)
    grad_v = mm(weights_b, g, 1, 0)
    grad_k = mm(dscores_b, q, 1, 0) * factor
    grad_q = mm(dscores_b, k, 0, 0) * factor
    return grad_q, grad_k, grad_v


def own_kernel(blocks, heads, factor, pack_ref, k_ref, v_ref, dq_ref, dk_ref, dv_ref):
    rows = blocks * BLOCK
    key_at = lax.broadcasted_iota(jnp.int32, (BLOCK, BLOCK), 0)
    query_at = lax.broadcasted_iota(jnp.int32, (BLOCK, BLOCK), 1)
    keep = key_at <= query_at
    for b in range(blocks):
        for h in range(heads):
            at = slice(b * BLOCK, (b + 1) * BLOCK)
            cols = slice(h * BLOCK, (h + 1) * BLOCK)
            norm, delta = stat_lines(pack_ref[2 * rows :, cols], b)
            grad_q, grad_k, grad_v = pair_terms(
                pack_ref[at, cols],
                pack_ref[rows + b * BLOCK : rows + (b + 1) * BLOCK, cols],
                k_ref[at, cols],
                v_ref[at, cols],
                norm,
                delta,
                factor,
                keep,
            )
            dq_ref[at, cols] = grad_q
            dk_ref[at, cols] = grad_k
            dv_ref[at, cols] = grad_v


def remote_kernel(blocks, factor, slots_ref, pack_ref, kv_ref, dq_ref, dkv_ref, acc_ref, line_ref):
    rows = blocks * BLOCK
    dq_ref[...] = jnp.zeros_like(dq_ref)
    acc_ref[...] = jnp.zeros_like(acc_ref)
    count = slots_ref[0]

    def turn(step, carry):
        done = []
        for u in range(UNROLL):
            slot = step * UNROLL + u
            code = slots_ref[1 + jnp.minimum(slot, count - 1)]
            live = slot < count
            kb = code % blocks
            kx = code // blocks % X_SIZE
            h = code // (blocks * X_SIZE) % 4
            b = code // (blocks * X_SIZE * 4) % blocks
            zq = code // (blocks * X_SIZE * 4 * blocks)
            cols = pl.ds(pl.multiple_of(h * BLOCK, BLOCK), BLOCK)
            q_at = pl.ds(pl.multiple_of(b * BLOCK, BLOCK), BLOCK)
            g_at = pl.ds(pl.multiple_of(rows + b * BLOCK, BLOCK), BLOCK)
            k_at = pl.ds(pl.multiple_of(kb * BLOCK, BLOCK), BLOCK)
            v_at = pl.ds(pl.multiple_of(rows + kb * BLOCK, BLOCK), BLOCK)
            norm, delta = stat_lines(pack_ref[zq, 2 * rows :, cols], b)
            terms = pair_terms(
                pack_ref[zq, q_at, cols],
                pack_ref[zq, g_at, cols],
                kv_ref[kx, k_at, cols],
                kv_ref[kx, v_at, cols],
                norm,
                delta,
                factor,
                live,
            )
            done.append((slot, code, zq, q_at, cols, kx, k_at, v_at, terms))
        for slot, code, zq, q_at, cols, kx, k_at, v_at, (grad_q, grad_k, grad_v) in done:
            acc_ref[kx, k_at, cols] += grad_k
            acc_ref[kx, v_at, cols] += grad_v
            before = slots_ref[1 + jnp.clip(slot - 1, 0, count - 1)]
            span = blocks * X_SIZE
            same = (slot > 0) & (before // span == code // span)
            total = jnp.where(same, line_ref[...], 0.0) + grad_q
            line_ref[...] = total
            dq_ref[zq, q_at, cols] = total.astype(BF16)
        return carry

    lax.fori_loop(0, (count + UNROLL - 1) // UNROLL, turn, 0)
    dkv_ref[...] = acc_ref[...].astype(BF16)


def slot_codes(table, plane, blocks):
    z_count, block_count, heads, top_count = table.shape
    slot_total = z_count * X_SIZE * PER_PEER
    span = blocks * X_SIZE
    flat = table.reshape(-1)
    total = flat.shape[0]
    ids = jnp.arange(total, dtype=jnp.int32)
    hit = (flat >= 0) & (flat // span == plane)
    code = (ids // top_count) * span + flat % span
    earlier = (ids[None, :] <= ids[:, None]) & hit[None, :]
    place = jnp.sum(earlier.astype(jnp.int32), axis=1) - 1
    match = (place[None, :] == jnp.arange(slot_total, dtype=jnp.int32)[:, None]) & hit[None, :]
    codes = jnp.sum(jnp.where(match, code[None, :], 0), axis=1)
    return jnp.concatenate([jnp.sum(hit.astype(jnp.int32))[None], codes])


def shards(queries, keys, values, out_grad, outputs, log_norms, selected):
    blocks, heads, top_count = selected.shape
    rows, width = queries.shape
    factor = (width // heads) ** (-0.5)
    z_count = lax.axis_size("z")
    x_count = lax.axis_size("x")
    params = pltpu.CompilerParams(vmem_limit_bytes=56 * 1024 * 1024)
    pack = pl.pallas_call(
        functools.partial(pack_kernel, blocks, heads),
        out_shape=jax.ShapeDtypeStruct((2 * rows + STAT_ROWS, width), BF16),
        compiler_params=params,
        name="pack",
    )(queries, out_grad, outputs, log_norms)
    packs = lax.all_gather(pack, "z")
    table = lax.all_to_all(
        jnp.broadcast_to(selected[None], (z_count, *selected.shape)), "z", 0, 0, tiled=True
    )
    both = jnp.concatenate([keys, values], axis=0)
    kvs = lax.all_to_all(
        jnp.broadcast_to(both[None], (x_count, *both.shape)), "x", 0, 0, tiled=True
    )
    own = jax.ShapeDtypeStruct((rows, width), F32)
    own_q, own_k, own_v = pl.pallas_call(
        functools.partial(own_kernel, blocks, heads, factor),
        out_shape=(own, own, own),
        compiler_params=params,
        name="own",
    )(pack, keys, values)
    codes = slot_codes(table, lax.axis_index("z"), blocks)
    part_q, part_kv = pl.pallas_call(
        functools.partial(remote_kernel, blocks, factor),
        in_specs=[
            pl.BlockSpec(memory_space=pltpu.SMEM),
            pl.BlockSpec(memory_space=pltpu.VMEM),
            pl.BlockSpec(memory_space=pltpu.VMEM),
        ],
        out_specs=(
            pl.BlockSpec(memory_space=pltpu.VMEM),
            pl.BlockSpec(memory_space=pltpu.VMEM),
        ),
        out_shape=(
            jax.ShapeDtypeStruct((z_count, rows, width), BF16),
            jax.ShapeDtypeStruct((x_count, 2 * rows, width), BF16),
        ),
        scratch_shapes=[
            pltpu.VMEM((x_count, 2 * rows, width), F32),
            pltpu.VMEM((BLOCK, BLOCK), F32),
        ],
        compiler_params=params,
        name="remote",
    )(codes, packs, kvs)
    sum_q = lax.psum_scatter(part_q, "z", scatter_dimension=0)
    back = lax.all_to_all(part_kv, "x", 0, 0, tiled=True).astype(F32)
    sum_kv = jnp.sum(back, axis=0)
    final_k = (sum_kv[:rows] + own_k).astype(BF16)
    final_v = (sum_kv[rows:] + own_v).astype(BF16)
    final_q = (sum_q.astype(F32) + own_q).astype(BF16)
    spread_q = lax.all_to_all(final_q, "head", split_axis=0, concat_axis=1, tiled=True)
    return spread_q, final_k, final_v


def solution(mesh):
    ctx_count, head_count = mesh.devices.shape
    grid = mesh.devices.reshape(ctx_count // X_SIZE, X_SIZE, head_count)
    fine = Mesh(grid, ("z", "x", "head"))
    placed = P(("z", "x"), "head")
    return jax.shard_map(
        shards,
        mesh=fine,
        in_specs=(placed,) * 6 + (P(("z", "x"), "head", None),),
        out_specs=(P(("z", "x", "head"), None), placed, placed),
        check_vma=False,
    )
```

```python
import functools

import jax
import jax.numpy as jnp
from jax import lax
from jax.experimental import pallas as pl
from jax.experimental.pallas import tpu as pltpu
from jax.sharding import Mesh
from jax.sharding import PartitionSpec as P

X_SIZE = 4
BLOCK = 128
STAT_ROWS = 16
PER_PEER = 2
PAIR = 2
UNROLL = 4
F32 = jnp.float32
BF16 = jnp.bfloat16


def mm(left, right, left_dim, right_dim):
    return lax.dot_general(
        left, right, (((left_dim,), (right_dim,)), ((), ())), preferred_element_type=F32
    )


def three_parts(value):
    high = value.astype(BF16)
    rest = value - high.astype(F32)
    middle = rest.astype(BF16)
    low = (rest - middle.astype(F32)).astype(BF16)
    return high, middle, low


def pack_kernel(blocks, heads, q_ref, g_ref, o_ref, n_ref, out_ref):
    rows = blocks * BLOCK
    out_ref[0:rows, :] = q_ref[...]
    out_ref[rows : 2 * rows, :] = g_ref[...]
    for h in range(heads):
        cols = slice(h * BLOCK, (h + 1) * BLOCK)
        lines = []
        for b in range(blocks):
            at = slice(b * BLOCK, (b + 1) * BLOCK)
            product = g_ref[at, cols].astype(F32) * o_ref[at, cols].astype(F32)
            delta = jnp.sum(product.T, axis=0, keepdims=True)
            norm = n_ref[h : h + 1, at]
            lines += list(three_parts(norm)) + list(three_parts(delta))
        lines = [line.astype(F32) for line in lines]
        pad = jnp.zeros((STAT_ROWS - len(lines), BLOCK), F32)
        out_ref[2 * rows :, cols] = jnp.concatenate(lines + [pad], axis=0).astype(BF16)


def stat_lines(tile, b):
    tile = tile.astype(F32)

    def line(at):
        return (tile[at : at + 1] + tile[at + 1 : at + 2]) + tile[at + 2 : at + 3]

    if isinstance(b, int):
        return line(6 * b), line(6 * b + 3)
    first = b == 0
    return jnp.where(first, line(0), line(6)), jnp.where(first, line(3), line(9))


def pair_terms(q, g, k, v, norm, delta, factor, keep):
    scores = mm(k, q, 1, 1) * factor
    weights = jnp.where(keep, jnp.exp(scores - norm), 0.0)
    dscores = weights * (mm(v, g, 1, 1) - delta)
    weights_b = weights.astype(BF16)
    dscores_b = dscores.astype(BF16)
    grad_v = mm(weights_b, g, 1, 0)
    grad_k = mm(dscores_b, q, 1, 0) * factor
    grad_q = mm(dscores_b, k, 0, 0) * factor
    return grad_q, grad_k, grad_v


def own_kernel(blocks, heads, factor, pack_ref, k_ref, v_ref, dq_ref, dk_ref, dv_ref):
    rows = blocks * BLOCK
    key_at = lax.broadcasted_iota(jnp.int32, (BLOCK, BLOCK), 0)
    query_at = lax.broadcasted_iota(jnp.int32, (BLOCK, BLOCK), 1)
    keep = key_at <= query_at
    for b in range(blocks):
        for h in range(heads):
            at = slice(b * BLOCK, (b + 1) * BLOCK)
            cols = slice(h * BLOCK, (h + 1) * BLOCK)
            norm, delta = stat_lines(pack_ref[2 * rows :, cols], b)
            grad_q, grad_k, grad_v = pair_terms(
                pack_ref[at, cols],
                pack_ref[rows + b * BLOCK : rows + (b + 1) * BLOCK, cols],
                k_ref[at, cols],
                v_ref[at, cols],
                norm,
                delta,
                factor,
                keep,
            )
            dq_ref[at, cols] = grad_q
            dk_ref[at, cols] = grad_k
            dv_ref[at, cols] = grad_v


def remote_kernel(blocks, heads, factor, owners, *refs):
    slots_ref, packs_ref, own_k_ref, own_v_ref = refs[:4]
    kv_refs = refs[4 : 4 + owners]
    dq_ref, near_ref = refs[4 + owners : 6 + owners]
    far_refs = refs[6 + owners : 5 + 2 * owners]
    acc_ref, line_ref, pack_ref, kv_ref, sems = refs[5 + 2 * owners :]
    rows = blocks * BLOCK
    span = blocks * owners
    loads = [pltpu.make_async_copy(packs_ref, pack_ref, sems.at[owners])]
    for at in range(owners):
        loads.append(pltpu.make_async_copy(kv_refs[at], kv_ref.at[at], sems.at[at]))
    for load in loads:
        load.start()
    dq_ref[...] = jnp.zeros_like(dq_ref)
    acc_ref[0, :rows] = own_k_ref[...]
    acc_ref[0, rows:] = own_v_ref[...]
    acc_ref[1:] = jnp.zeros((owners - 1, *acc_ref.shape[1:]), F32)
    count = slots_ref[0]
    for load in loads:
        load.wait()

    def turn(step, carry):
        done = []
        for u in range(UNROLL):
            slot = step * UNROLL + u
            code = slots_ref[1 + jnp.minimum(slot, count - 1)]
            live = slot < count
            kb = code % blocks
            kx = code // blocks % owners
            h = code // span % heads
            b = code // (span * heads) % blocks
            zq = code // (span * heads * blocks)
            cols = pl.ds(pl.multiple_of(h * BLOCK, BLOCK), BLOCK)
            q_at = pl.ds(pl.multiple_of(b * BLOCK, BLOCK), BLOCK)
            g_at = pl.ds(pl.multiple_of(rows + b * BLOCK, BLOCK), BLOCK)
            k_at = pl.ds(pl.multiple_of(kb * BLOCK, BLOCK), BLOCK)
            v_at = pl.ds(pl.multiple_of(rows + kb * BLOCK, BLOCK), BLOCK)
            norm, delta = stat_lines(pack_ref[zq, 2 * rows :, cols], b)
            terms = pair_terms(
                pack_ref[zq, q_at, cols],
                pack_ref[zq, g_at, cols],
                kv_ref[kx, k_at, cols],
                kv_ref[kx, v_at, cols],
                norm,
                delta,
                factor,
                live,
            )
            done.append((slot, code, zq, q_at, cols, kx, k_at, v_at, terms))
        for slot, code, zq, q_at, cols, kx, k_at, v_at, (grad_q, grad_k, grad_v) in done:
            acc_ref[kx, k_at, cols] += grad_k
            acc_ref[kx, v_at, cols] += grad_v
            before = slots_ref[1 + jnp.clip(slot - 1, 0, count - 1)]
            same = (slot > 0) & (before // span == code // span)
            total = jnp.where(same, line_ref[...], 0.0) + grad_q
            line_ref[...] = total
            dq_ref[zq, q_at, cols] = total.astype(BF16)
        return carry

    lax.fori_loop(0, (count + UNROLL - 1) // UNROLL, turn, 0)
    near_ref[...] = acc_ref[0]
    for at in range(1, owners):
        far_refs[at - 1][...] = acc_ref[at].astype(BF16)


def slot_codes(table, j, p, x, owners):
    ring, blocks, heads, top_count = table.shape
    slot_total = ring * owners * PER_PEER
    span = blocks * owners
    flat = table.reshape(-1)
    ids = jnp.arange(flat.shape[0], dtype=jnp.int32)
    hit = (flat >= 0) & (flat // span == j)
    owner = flat % span // blocks
    near = (owner % X_SIZE - x) % X_SIZE * PAIR + (owner // X_SIZE - p) % PAIR
    code = ids // top_count * span + near * blocks + flat % blocks
    earlier = (ids[None, :] <= ids[:, None]) & hit[None, :]
    place = jnp.sum(earlier.astype(jnp.int32), axis=1) - 1
    match = (place[None, :] == jnp.arange(slot_total, dtype=jnp.int32)[:, None]) & hit[None, :]
    codes = jnp.sum(jnp.where(match, code[None, :], 0), axis=1)
    return jnp.concatenate([jnp.sum(hit.astype(jnp.int32))[None], codes])


def shards(queries, keys, values, out_grad, outputs, log_norms, selected):
    blocks, heads, top_count = selected.shape
    rows, width = queries.shape
    factor = (width // heads) ** (-0.5)
    ring = lax.axis_size("j")
    owners = lax.axis_size("p") * lax.axis_size("x")
    params = pltpu.CompilerParams(vmem_limit_bytes=56 * 1024 * 1024)
    pack = pl.pallas_call(
        functools.partial(pack_kernel, blocks, heads),
        out_shape=jax.ShapeDtypeStruct((2 * rows + STAT_ROWS, width), BF16),
        compiler_params=params,
        name="pack",
    )(queries, out_grad, outputs, log_norms.T)
    packs = lax.all_gather(pack, "j")
    pack, selected, keys, values = lax.optimization_barrier((pack, selected, keys, values))
    table = lax.all_to_all(
        jnp.broadcast_to(selected[None], (ring, *selected.shape)), "j", 0, 0, tiled=True
    )
    both = jnp.concatenate([keys, values], axis=0)
    swapped = lax.ppermute(both, "p", [(i, (i + 1) % PAIR) for i in range(PAIR)])
    kvs = [both, swapped]
    for shift in range(1, X_SIZE):
        back = [(i, (i - shift) % X_SIZE) for i in range(X_SIZE)]
        kvs += [lax.ppermute(both, "x", back), lax.ppermute(swapped, "x", back)]
    own = jax.ShapeDtypeStruct((rows, width), F32)
    own_q, own_k, own_v = pl.pallas_call(
        functools.partial(own_kernel, blocks, heads, factor),
        out_shape=(own, own, own),
        compiler_params=params,
        name="own",
    )(pack, keys, values)
    codes = slot_codes(table, lax.axis_index("j"), lax.axis_index("p"), lax.axis_index("x"), owners)
    packs, kvs, codes, own_q, own_k, own_v = lax.optimization_barrier(
        (packs, kvs, codes, own_q, own_k, own_v)
    )
    anywhere = pl.BlockSpec(memory_space=pl.ANY)
    vmem = pl.BlockSpec(memory_space=pltpu.VMEM)
    part_q, near, *far = pl.pallas_call(
        functools.partial(remote_kernel, blocks, heads, factor, owners),
        in_specs=[pl.BlockSpec(memory_space=pltpu.SMEM), anywhere, vmem, vmem] + [anywhere] * owners,
        out_specs=(vmem,) * (owners + 1),
        out_shape=(
            jax.ShapeDtypeStruct((ring, rows, width), BF16),
            jax.ShapeDtypeStruct((2 * rows, width), F32),
        )
        + (jax.ShapeDtypeStruct((2 * rows, width), BF16),) * (owners - 1),
        scratch_shapes=[
            pltpu.VMEM((owners, 2 * rows, width), F32),
            pltpu.VMEM((BLOCK, BLOCK), F32),
            pltpu.VMEM((ring, 2 * rows + STAT_ROWS, width), BF16),
            pltpu.VMEM((owners, 2 * rows, width), BF16),
            pltpu.SemaphoreType.DMA((owners + 1,)),
        ],
        compiler_params=params,
        name="remote",
    )(codes, packs, own_k, own_v, *kvs)
    sum_q = lax.psum_scatter(part_q, "j", scatter_dimension=0)
    sum_kv = near
    for at in range(1, owners):
        shift, other = at // PAIR, at % PAIR
        pairs = [
            (p * X_SIZE + x, (p + other) % PAIR * X_SIZE + (x + shift) % X_SIZE)
            for p in range(PAIR)
            for x in range(X_SIZE)
        ]
        sum_kv = sum_kv + lax.ppermute(far[at - 1], ("p", "x"), pairs).astype(F32)
    final_k = sum_kv[:rows].astype(BF16)
    final_v = sum_kv[rows:].astype(BF16)
    sum_q, final_k, final_v = lax.optimization_barrier((sum_q, final_k, final_v))
    final_q = (sum_q.astype(F32) + own_q).astype(BF16)
    spread_q = lax.all_to_all(final_q, "head", split_axis=0, concat_axis=1, tiled=True)
    return spread_q, final_k, final_v


def solution(mesh):
    ctx_count, head_count = mesh.devices.shape
    grid = mesh.devices.reshape(ctx_count // (PAIR * X_SIZE), PAIR, X_SIZE, head_count)
    fine = Mesh(grid, ("j", "p", "x", "head"))
    ctx = ("j", "p", "x")
    placed = P(ctx, "head")
    return jax.shard_map(
        shards,
        mesh=fine,
        in_specs=(placed,) * 6 + (P(ctx, "head", None),),
        out_specs=(P((*ctx, "head"), None), placed, placed),
        check_vma=False,
    )
```

```python
import functools

import jax
import jax.numpy as jnp
from jax import lax
from jax.experimental import pallas as pl
from jax.experimental.pallas import tpu as pltpu
from jax.sharding import Mesh
from jax.sharding import PartitionSpec as P

X_SIZE = 4
BLOCK = 128
STAT_ROWS = 16
PER_PEER = 2
PAIR = 2
UNROLL = 4
F32 = jnp.float32
BF16 = jnp.bfloat16
PARAMS = pltpu.CompilerParams(vmem_limit_bytes=56 * 1024 * 1024)


def mm(left, right, left_dim, right_dim):
    return lax.dot_general(
        left, right, (((left_dim,), (right_dim,)), ((), ())), preferred_element_type=F32
    )


def three_parts(value):
    high = value.astype(BF16)
    rest = value - high.astype(F32)
    middle = rest.astype(BF16)
    low = (rest - middle.astype(F32)).astype(BF16)
    return high, middle, low


def pack_kernel(blocks, heads, q_ref, g_ref, o_ref, n_ref, out_ref):
    rows = blocks * BLOCK
    out_ref[0:rows, :] = q_ref[...]
    out_ref[rows : 2 * rows, :] = g_ref[...]
    for h in range(heads):
        cols = slice(h * BLOCK, (h + 1) * BLOCK)
        lines = []
        for b in range(blocks):
            at = slice(b * BLOCK, (b + 1) * BLOCK)
            product = g_ref[at, cols].astype(F32) * o_ref[at, cols].astype(F32)
            delta = jnp.sum(product.T, axis=0, keepdims=True)
            norm = n_ref[h : h + 1, at]
            lines += list(three_parts(norm)) + list(three_parts(delta))
        lines = [line.astype(F32) for line in lines]
        pad = jnp.zeros((STAT_ROWS - len(lines), BLOCK), F32)
        out_ref[2 * rows :, cols] = jnp.concatenate(lines + [pad], axis=0).astype(BF16)


def stat_lines(tile, b):
    tile = tile.astype(F32)

    def line(at):
        return (tile[at : at + 1] + tile[at + 1 : at + 2]) + tile[at + 2 : at + 3]

    if isinstance(b, int):
        return line(6 * b), line(6 * b + 3)
    first = b == 0
    return jnp.where(first, line(0), line(6)), jnp.where(first, line(3), line(9))


def pair_terms(q, g, k, v, norm, delta, factor, keep):
    scores = mm(k, q, 1, 1) * factor
    weights = jnp.where(keep, jnp.exp(scores - norm), 0.0)
    dscores = weights * (mm(v, g, 1, 1) - delta)
    weights_b = weights.astype(BF16)
    dscores_b = dscores.astype(BF16)
    grad_v = mm(weights_b, g, 1, 0)
    grad_k = mm(dscores_b, q, 1, 0) * factor
    grad_q = mm(dscores_b, k, 0, 0) * factor
    return grad_q, grad_k, grad_v


def own_kernel(blocks, heads, factor, pack_ref, k_ref, v_ref, dq_ref, dk_ref, dv_ref):
    rows = blocks * BLOCK
    key_at = lax.broadcasted_iota(jnp.int32, (BLOCK, BLOCK), 0)
    query_at = lax.broadcasted_iota(jnp.int32, (BLOCK, BLOCK), 1)
    keep = key_at <= query_at
    for b in range(blocks):
        for h in range(heads):
            at = slice(b * BLOCK, (b + 1) * BLOCK)
            cols = slice(h * BLOCK, (h + 1) * BLOCK)
            norm, delta = stat_lines(pack_ref[2 * rows :, cols], b)
            grad_q, grad_k, grad_v = pair_terms(
                pack_ref[at, cols],
                pack_ref[rows + b * BLOCK : rows + (b + 1) * BLOCK, cols],
                k_ref[at, cols],
                v_ref[at, cols],
                norm,
                delta,
                factor,
                keep,
            )
            dq_ref[at, cols] = grad_q
            dk_ref[at, cols] = grad_k
            dv_ref[at, cols] = grad_v


def low_bits(value, size):
    return value & (size - 1), value >> (size.bit_length() - 1)


def remote_kernel(blocks, heads, factor, owners, *refs):
    slots_ref, packs_ref, own_k_ref, own_v_ref = refs[:4]
    kv_refs = refs[4 : 4 + owners]
    dq_out, near_out = refs[4 + owners : 6 + owners]
    far_outs = refs[6 + owners : 5 + owners + owners // PAIR]
    dq_ref, acc_ref, far_ref, line_ref, pack_ref, kv_ref, sems = refs[5 + owners + owners // PAIR :]
    rows = blocks * BLOCK
    span = blocks * owners
    loads = [pltpu.make_async_copy(packs_ref, pack_ref, sems.at[owners])]
    for at in range(owners):
        loads.append(pltpu.make_async_copy(kv_refs[at], kv_ref.at[at], sems.at[at]))
    for load in loads:
        load.start()
    dq_ref[...] = jnp.zeros_like(dq_ref)
    acc_ref[0, :rows] = own_k_ref[...]
    acc_ref[0, rows:] = own_v_ref[...]
    acc_ref[1:] = jnp.zeros((owners - 1, *acc_ref.shape[1:]), F32)
    count = slots_ref[0]
    for load in loads:
        load.wait()

    def turn(step, carry):
        done = []
        for u in range(UNROLL):
            slot = step * UNROLL + u
            live = slot < count
            code = slots_ref[1 + jnp.where(live, slot, count - 1)]
            kb, rest = low_bits(code, blocks)
            kx, rest = low_bits(rest, owners)
            h, rest = low_bits(rest, heads)
            b, zq = low_bits(rest, blocks)
            cols = pl.ds(pl.multiple_of(h * BLOCK, BLOCK), BLOCK)
            q_at = pl.ds(pl.multiple_of(b * BLOCK, BLOCK), BLOCK)
            g_at = pl.ds(pl.multiple_of(rows + b * BLOCK, BLOCK), BLOCK)
            k_at = pl.ds(pl.multiple_of(kb * BLOCK, BLOCK), BLOCK)
            v_at = pl.ds(pl.multiple_of(rows + kb * BLOCK, BLOCK), BLOCK)
            norm, delta = stat_lines(pack_ref[zq, 2 * rows :, cols], b)
            terms = pair_terms(
                pack_ref[zq, q_at, cols],
                pack_ref[zq, g_at, cols],
                kv_ref[kx, k_at, cols],
                kv_ref[kx, v_at, cols],
                norm,
                delta,
                factor,
                live,
            )
            before = slots_ref[jnp.where(live, slot, count)]
            shift = span.bit_length() - 1
            same = (slot > 0) & ((before >> shift) == (code >> shift))
            done.append((same, zq, q_at, cols, kx, k_at, v_at, terms))
        for same, zq, q_at, cols, kx, k_at, v_at, (grad_q, grad_k, grad_v) in done:
            acc_ref[kx, k_at, cols] += grad_k
            acc_ref[kx, v_at, cols] += grad_v
            total = jnp.where(same, line_ref[...], 0.0) + grad_q
            line_ref[...] = total
            dq_ref[zq, q_at, cols] = total.astype(BF16)
        return carry

    lax.fori_loop(0, (count + UNROLL - 1) // UNROLL, turn, 0)
    stores = [
        pltpu.make_async_copy(dq_ref, dq_out, sems.at[0]),
        pltpu.make_async_copy(acc_ref.at[pl.ds(0, PAIR)], near_out, sems.at[1]),
    ]
    for store in stores:
        store.start()
    for at in range(PAIR, owners):
        far_ref[at - PAIR] = acc_ref[at].astype(BF16)
        if at % PAIR == PAIR - 1:
            first = at - 2 * PAIR + 1
            turned = pltpu.make_async_copy(
                far_ref.at[pl.ds(first, PAIR)], far_outs[first // PAIR], sems.at[at]
            )
            turned.start()
            stores.append(turned)
    for store in stores:
        store.wait()


def slot_codes(table, j, p, x, owners):
    ring, blocks, heads, top_count = table.shape
    slot_total = ring * owners * PER_PEER
    span = blocks * owners
    flat = table.reshape(-1)
    ids = jnp.arange(flat.shape[0], dtype=jnp.int32)
    hit = (flat >= 0) & (flat // span == j)
    owner = flat % span // blocks
    near = (owner % X_SIZE - x) % X_SIZE * PAIR + (owner // X_SIZE - p) % PAIR
    code = ids // top_count * span + near * blocks + flat % blocks
    earlier = (ids[None, :] <= ids[:, None]) & hit[None, :]
    place = jnp.sum(earlier.astype(jnp.int32), axis=1) - 1
    match = (place[None, :] == jnp.arange(slot_total, dtype=jnp.int32)[:, None]) & hit[None, :]
    codes = jnp.sum(jnp.where(match, code[None, :], 0), axis=1)
    return jnp.concatenate([jnp.sum(hit.astype(jnp.int32))[None], codes])


def remote_call(codes, packs, own_k, own_v, kvs, blocks, heads, factor, rows, width, ring, owners):
    anywhere = pl.BlockSpec(memory_space=pl.ANY)
    vmem = pl.BlockSpec(memory_space=pltpu.VMEM)
    return pl.pallas_call(
        functools.partial(remote_kernel, blocks, heads, factor, owners),
        in_specs=[pl.BlockSpec(memory_space=pltpu.SMEM), anywhere, vmem, vmem] + [anywhere] * owners,
        out_specs=(anywhere,) * (X_SIZE + 1),
        out_shape=(
            jax.ShapeDtypeStruct((ring, rows, width), BF16),
            jax.ShapeDtypeStruct((PAIR, 2 * rows, width), F32),
        )
        + (jax.ShapeDtypeStruct((PAIR, 2 * rows, width), BF16),) * (X_SIZE - 1),
        scratch_shapes=[
            pltpu.VMEM((ring, rows, width), BF16),
            pltpu.VMEM((owners, 2 * rows, width), F32),
            pltpu.VMEM((owners - PAIR, 2 * rows, width), BF16),
            pltpu.VMEM((BLOCK, BLOCK), F32),
            pltpu.VMEM((ring, 2 * rows + STAT_ROWS, width), BF16),
            pltpu.VMEM((owners, 2 * rows, width), BF16),
            pltpu.SemaphoreType.DMA((owners + 1,)),
        ],
        compiler_params=PARAMS,
        name="remote",
    )(codes, packs, own_k, own_v, *kvs)


def shards(queries, keys, values, out_grad, outputs, log_norms, selected):
    blocks, heads, top_count = selected.shape
    rows, width = queries.shape
    factor = (width // heads) ** (-0.5)
    ring = lax.axis_size("j")
    owners = lax.axis_size("p") * lax.axis_size("x")
    pack = pl.pallas_call(
        functools.partial(pack_kernel, blocks, heads),
        out_shape=jax.ShapeDtypeStruct((2 * rows + STAT_ROWS, width), BF16),
        compiler_params=PARAMS,
        name="pack",
    )(queries, out_grad, outputs, log_norms.T)
    packs = lax.all_gather(pack, "j")
    pack, selected, keys, values = lax.optimization_barrier((pack, selected, keys, values))
    table = lax.all_to_all(
        jnp.broadcast_to(selected[None], (ring, *selected.shape)), "j", 0, 0, tiled=True
    )
    both = jnp.concatenate([keys, values], axis=0)
    swapped = lax.ppermute(both, "p", [(i, (i + 1) % PAIR) for i in range(PAIR)])
    kvs = [both, swapped]
    for shift in range(1, X_SIZE):
        back = [(i, (i - shift) % X_SIZE) for i in range(X_SIZE)]
        kvs += [lax.ppermute(both, "x", back), lax.ppermute(swapped, "x", back)]
    own = jax.ShapeDtypeStruct((rows, width), F32)
    own_q, own_k, own_v = pl.pallas_call(
        functools.partial(own_kernel, blocks, heads, factor),
        out_shape=(own, own, own),
        compiler_params=PARAMS,
        name="own",
    )(pack, keys, values)
    codes = slot_codes(table, lax.axis_index("j"), lax.axis_index("p"), lax.axis_index("x"), owners)
    packs, kvs, codes, own_q, own_k, own_v = lax.optimization_barrier(
        (packs, kvs, codes, own_q, own_k, own_v)
    )
    part_q, near, *far = remote_call(
        codes, packs, own_k, own_v, kvs, blocks, heads, factor, rows, width, ring, owners
    )
    sum_q = lax.psum_scatter(part_q, "j", scatter_dimension=0)
    sum_kv = near
    for shift in range(1, X_SIZE):
        ahead = [(i, (i + shift) % X_SIZE) for i in range(X_SIZE)]
        sum_kv = sum_kv + lax.ppermute(far[shift - 1], "x", ahead).astype(F32)
    crossed = lax.ppermute(sum_kv[1].astype(BF16), "p", [(i, (i + 1) % PAIR) for i in range(PAIR)])
    final_kv = sum_kv[0] + crossed.astype(F32)
    final_k = final_kv[:rows].astype(BF16)
    final_v = final_kv[rows:].astype(BF16)
    final_q = (sum_q.astype(F32) + own_q).astype(BF16)
    spread_q = lax.all_to_all(final_q, "head", split_axis=0, concat_axis=1, tiled=True)
    return spread_q, final_k, final_v


def solution(mesh):
    ctx_count, head_count = mesh.devices.shape
    grid = mesh.devices.reshape(ctx_count // (PAIR * X_SIZE), PAIR, X_SIZE, head_count)
    fine = Mesh(grid, ("j", "p", "x", "head"))
    ctx = ("j", "p", "x")
    placed = P(ctx, "head")
    return jax.shard_map(
        shards,
        mesh=fine,
        in_specs=(placed,) * 6 + (P(ctx, "head", None),),
        out_specs=(P((*ctx, "head"), None), placed, placed),
        check_vma=False,
    )
```

```python
import functools

import jax
import jax.numpy as jnp
from jax import lax
from jax.experimental import pallas as pl
from jax.experimental.pallas import tpu as pltpu
from jax.sharding import Mesh
from jax.sharding import PartitionSpec as P

X_SIZE = 4
BLOCK = 128
STAT_ROWS = 16
PER_PEER = 2
PAIR = 2
UNROLL = 8
F32 = jnp.float32
BF16 = jnp.bfloat16
PARAMS = pltpu.CompilerParams(vmem_limit_bytes=56 * 1024 * 1024)


def mm(left, right, left_dim, right_dim):
    return lax.dot_general(
        left, right, (((left_dim,), (right_dim,)), ((), ())), preferred_element_type=F32
    )


def three_parts(value):
    high = value.astype(BF16)
    rest = value - high.astype(F32)
    middle = rest.astype(BF16)
    low = (rest - middle.astype(F32)).astype(BF16)
    return high, middle, low


def pack_kernel(blocks, heads, q_ref, g_ref, o_ref, n_ref, out_ref):
    rows = blocks * BLOCK
    out_ref[0:rows, :] = q_ref[...]
    out_ref[rows : 2 * rows, :] = g_ref[...]
    for h in range(heads):
        cols = slice(h * BLOCK, (h + 1) * BLOCK)
        lines = []
        for b in range(blocks):
            at = slice(b * BLOCK, (b + 1) * BLOCK)
            product = g_ref[at, cols].astype(F32) * o_ref[at, cols].astype(F32)
            delta = jnp.sum(product.T, axis=0, keepdims=True)
            norm = n_ref[h : h + 1, at]
            lines += list(three_parts(norm)) + list(three_parts(delta))
        lines = [line.astype(F32) for line in lines]
        pad = jnp.zeros((STAT_ROWS - len(lines), BLOCK), F32)
        out_ref[2 * rows :, cols] = jnp.concatenate(lines + [pad], axis=0).astype(BF16)


def stat_lines(tile, b):
    tile = tile.astype(F32)

    def line(at):
        return (tile[at : at + 1] + tile[at + 1 : at + 2]) + tile[at + 2 : at + 3]

    if isinstance(b, int):
        return line(6 * b), line(6 * b + 3)
    first = b == 0
    return jnp.where(first, line(0), line(6)), jnp.where(first, line(3), line(9))


def pair_terms(q, g, k, v, norm, delta, factor, keep):
    blank = jnp.zeros_like(q)
    queries = jnp.concatenate(
        [jnp.concatenate([q, blank], axis=1), jnp.concatenate([blank, g], axis=1)], axis=0
    )
    products = mm(jnp.concatenate([k, v], axis=1), queries, 1, 1)
    scores = products[:, :BLOCK] * factor
    weights = jnp.where(keep, jnp.exp(scores - norm), 0.0)
    dscores = weights * (products[:, BLOCK:] - delta)
    weights_b = weights.astype(BF16)
    dscores_b = dscores.astype(BF16)
    grads = mm(jnp.concatenate([dscores_b, weights_b], axis=1), queries, 1, 0)
    grad_q = mm(dscores_b, k, 0, 0) * factor
    return grad_q, grads[:, :BLOCK] * factor, grads[:, BLOCK:]


def own_kernel(blocks, heads, factor, pack_ref, k_ref, v_ref, dq_ref, dk_ref, dv_ref):
    rows = blocks * BLOCK
    key_at = lax.broadcasted_iota(jnp.int32, (BLOCK, BLOCK), 0)
    query_at = lax.broadcasted_iota(jnp.int32, (BLOCK, BLOCK), 1)
    keep = key_at <= query_at
    for b in range(blocks):
        for h in range(heads):
            at = slice(b * BLOCK, (b + 1) * BLOCK)
            cols = slice(h * BLOCK, (h + 1) * BLOCK)
            norm, delta = stat_lines(pack_ref[2 * rows :, cols], b)
            grad_q, grad_k, grad_v = pair_terms(
                pack_ref[at, cols],
                pack_ref[rows + b * BLOCK : rows + (b + 1) * BLOCK, cols],
                k_ref[at, cols],
                v_ref[at, cols],
                norm,
                delta,
                factor,
                keep,
            )
            dq_ref[at, cols] = grad_q
            dk_ref[at, cols] = grad_k
            dv_ref[at, cols] = grad_v


def low_bits(value, size):
    return value & (size - 1), value >> (size.bit_length() - 1)


def remote_kernel(blocks, heads, factor, owners, *refs):
    slots_ref, packs_ref, own_k_ref, own_v_ref = refs[:4]
    kv_refs = refs[4 : 4 + owners]
    dq_out, *part_outs = refs[4 + owners : 5 + 2 * owners]
    dq_ref, acc_ref, far_ref, line_ref, pack_ref, kv_ref, sems = refs[5 + 2 * owners :]
    rows = blocks * BLOCK
    span = blocks * owners
    loads = [
        pltpu.make_async_copy(packs_ref, pack_ref, sems.at[owners]),
        pltpu.make_async_copy(own_k_ref, acc_ref.at[0, pl.ds(0, rows)], sems.at[owners + 1]),
        pltpu.make_async_copy(own_v_ref, acc_ref.at[0, pl.ds(rows, rows)], sems.at[owners + 2]),
    ]
    for at in range(owners):
        loads.append(pltpu.make_async_copy(kv_refs[at], kv_ref.at[at], sems.at[at]))
    for load in loads:
        load.start()
    dq_ref[...] = jnp.zeros_like(dq_ref)
    acc_ref[1:] = jnp.zeros((owners - 1, *acc_ref.shape[1:]), F32)
    count = slots_ref[0]
    for load in loads:
        load.wait()

    def turn(step, carry):
        done = []
        for u in range(UNROLL):
            slot = step * UNROLL + u
            live = slot < count
            code = slots_ref[1 + jnp.where(live, slot, count - 1)]
            kb, rest = low_bits(code, blocks)
            kx, rest = low_bits(rest, owners)
            h, rest = low_bits(rest, heads)
            b, zq = low_bits(rest, blocks)
            cols = pl.ds(pl.multiple_of(h * BLOCK, BLOCK), BLOCK)
            q_at = pl.ds(pl.multiple_of(b * BLOCK, BLOCK), BLOCK)
            g_at = pl.ds(pl.multiple_of(rows + b * BLOCK, BLOCK), BLOCK)
            k_at = pl.ds(pl.multiple_of(kb * BLOCK, BLOCK), BLOCK)
            v_at = pl.ds(pl.multiple_of(rows + kb * BLOCK, BLOCK), BLOCK)
            norm, delta = stat_lines(pack_ref[zq, 2 * rows :, cols], b)
            terms = pair_terms(
                pack_ref[zq, q_at, cols],
                pack_ref[zq, g_at, cols],
                kv_ref[kx, k_at, cols],
                kv_ref[kx, v_at, cols],
                norm,
                delta,
                factor,
                live,
            )
            before = slots_ref[jnp.where(live, slot, count)]
            shift = span.bit_length() - 1
            same = (slot > 0) & ((before >> shift) == (code >> shift))
            done.append((same, zq, q_at, cols, kx, k_at, v_at, terms))
        for same, zq, q_at, cols, kx, k_at, v_at, (grad_q, grad_k, grad_v) in done:
            acc_ref[kx, k_at, cols] += grad_k
            acc_ref[kx, v_at, cols] += grad_v
            total = jnp.where(same, line_ref[...], 0.0) + grad_q
            line_ref[...] = total
            dq_ref[zq, q_at, cols] = total.astype(BF16)
        return carry

    lax.fori_loop(0, (count + UNROLL - 1) // UNROLL, turn, 0)
    stores = [pltpu.make_async_copy(dq_ref, dq_out, sems.at[owners])]
    for at in range(PAIR):
        stores.append(pltpu.make_async_copy(acc_ref.at[at], part_outs[at], sems.at[at]))
    for store in stores:
        store.start()
    for at in range(PAIR, owners):
        far_ref[at - PAIR] = acc_ref[at].astype(BF16)
        turned = pltpu.make_async_copy(far_ref.at[at - PAIR], part_outs[at], sems.at[at])
        turned.start()
        stores.append(turned)
    for store in stores:
        store.wait()


def slot_codes(table, j, p, x, owners):
    ring, blocks, heads, top_count = table.shape
    slot_total = ring * owners * PER_PEER
    span = blocks * owners
    flat = table.reshape(-1)
    ids = jnp.arange(flat.shape[0], dtype=jnp.int32)
    hit = (flat >= 0) & (flat // span == j)
    owner = flat % span // blocks
    near = (owner % X_SIZE - x) % X_SIZE * PAIR + (owner // X_SIZE - p) % PAIR
    code = ids // top_count * span + near * blocks + flat % blocks
    earlier = (ids[None, :] <= ids[:, None]) & hit[None, :]
    place = jnp.sum(earlier.astype(jnp.int32), axis=1) - 1
    match = (place[None, :] == jnp.arange(slot_total, dtype=jnp.int32)[:, None]) & hit[None, :]
    codes = jnp.sum(jnp.where(match, code[None, :], 0), axis=1)
    return jnp.concatenate([jnp.sum(hit.astype(jnp.int32))[None], codes])


def remote_call(codes, packs, own_k, own_v, kvs, blocks, heads, factor, rows, width, ring, owners):
    anywhere = pl.BlockSpec(memory_space=pl.ANY)
    part = (2 * rows, width)
    return pl.pallas_call(
        functools.partial(remote_kernel, blocks, heads, factor, owners),
        in_specs=[pl.BlockSpec(memory_space=pltpu.SMEM)] + [anywhere] * (3 + owners),
        out_specs=(anywhere,) * (1 + owners),
        out_shape=(jax.ShapeDtypeStruct((ring, rows, width), BF16),)
        + (jax.ShapeDtypeStruct(part, F32),) * PAIR
        + (jax.ShapeDtypeStruct(part, BF16),) * (owners - PAIR),
        scratch_shapes=[
            pltpu.VMEM((ring, rows, width), BF16),
            pltpu.VMEM((owners, *part), F32),
            pltpu.VMEM((owners - PAIR, *part), BF16),
            pltpu.VMEM((BLOCK, BLOCK), F32),
            pltpu.VMEM((ring, 2 * rows + STAT_ROWS, width), BF16),
            pltpu.VMEM((owners, *part), BF16),
            pltpu.SemaphoreType.DMA((owners + 3,)),
        ],
        compiler_params=PARAMS,
        name="remote",
    )(codes, packs, own_k, own_v, *kvs)


def shards(queries, keys, values, out_grad, outputs, log_norms, selected):
    blocks, heads, top_count = selected.shape
    rows, width = queries.shape
    factor = (width // heads) ** (-0.5)
    ring = lax.axis_size("j")
    owners = lax.axis_size("p") * lax.axis_size("x")
    pack = pl.pallas_call(
        functools.partial(pack_kernel, blocks, heads),
        out_shape=jax.ShapeDtypeStruct((2 * rows + STAT_ROWS, width), BF16),
        compiler_params=PARAMS,
        name="pack",
    )(queries, out_grad, outputs, log_norms.T)
    packs = lax.all_gather(pack, "j")
    pack, selected, keys, values = lax.optimization_barrier((pack, selected, keys, values))
    table = lax.all_to_all(
        jnp.broadcast_to(selected[None], (ring, *selected.shape)), "j", 0, 0, tiled=True
    )
    both = jnp.concatenate([keys, values], axis=0)
    swapped = lax.ppermute(both, "p", [(i, (i + 1) % PAIR) for i in range(PAIR)])
    kvs = [both, swapped]
    for shift in range(1, X_SIZE):
        back = [(i, (i - shift) % X_SIZE) for i in range(X_SIZE)]
        kvs += [lax.ppermute(both, "x", back), lax.ppermute(swapped, "x", back)]
    own = jax.ShapeDtypeStruct((rows, width), F32)
    own_q, own_k, own_v = pl.pallas_call(
        functools.partial(own_kernel, blocks, heads, factor),
        out_shape=(own, own, own),
        compiler_params=PARAMS,
        name="own",
    )(pack, keys, values)
    codes = slot_codes(table, lax.axis_index("j"), lax.axis_index("p"), lax.axis_index("x"), owners)
    packs, kvs, codes, own_q, own_k, own_v = lax.optimization_barrier(
        (packs, kvs, codes, own_q, own_k, own_v)
    )
    part_q, near, near_other, next_a, next_b, far_a, far_b, last_a, last_b = remote_call(
        codes, packs, own_k, own_v, kvs, blocks, heads, factor, rows, width, ring, owners
    )
    sum_q = lax.psum_scatter(part_q, "j", scatter_dimension=0)
    ahead = [(i, (i + 1) % X_SIZE) for i in range(X_SIZE)]
    behind = [(i, (i - 1) % X_SIZE) for i in range(X_SIZE)]

    def wide(part):
        return part.astype(F32)

    through_a = lax.ppermute(far_a, "x", ahead)
    through_b = lax.ppermute(far_b, "x", behind)
    from_next = lax.ppermute(next_b, "x", ahead)
    from_last = lax.ppermute(last_a, "x", behind)
    next_a = (wide(next_a) + wide(through_a)).astype(BF16)
    last_b = (wide(last_b) + wide(through_b)).astype(BF16)
    sum_own = near + wide(from_last) + wide(lax.ppermute(next_a, "x", ahead))
    sum_other = near_other + wide(from_next) + wide(lax.ppermute(last_b, "x", behind))
    crossed = lax.ppermute(sum_other.astype(BF16), "p", [(i, (i + 1) % PAIR) for i in range(PAIR)])
    final_kv = sum_own + wide(crossed)
    final_k = final_kv[:rows].astype(BF16)
    final_v = final_kv[rows:].astype(BF16)
    final_q = (sum_q.astype(F32) + own_q).astype(BF16)
    spread_q = lax.all_to_all(final_q, "head", split_axis=0, concat_axis=1, tiled=True)
    return spread_q, final_k, final_v


def solution(mesh):
    ctx_count, head_count = mesh.devices.shape
    grid = mesh.devices.reshape(ctx_count // (PAIR * X_SIZE), PAIR, X_SIZE, head_count)
    fine = Mesh(grid, ("j", "p", "x", "head"))
    ctx = ("j", "p", "x")
    placed = P(ctx, "head")
    return jax.shard_map(
        shards,
        mesh=fine,
        in_specs=(placed,) * 6 + (P(ctx, "head", None),),
        out_specs=(P((*ctx, "head"), None), placed, placed),
        check_vma=False,
    )
```

```python
import functools

import jax
import jax.numpy as jnp
from jax import lax
from jax.experimental import pallas as pl
from jax.experimental.pallas import tpu as pltpu
from jax.sharding import Mesh
from jax.sharding import PartitionSpec as P

X_SIZE = 4
BLOCK = 128
PER_PEER = 2
PAIR = 2
UNROLL = 8
F32 = jnp.float32
BF16 = jnp.bfloat16
PARAMS = pltpu.CompilerParams(vmem_limit_bytes=56 * 1024 * 1024)


def mm(left, right, left_dim, right_dim):
    return lax.dot_general(
        left, right, (((left_dim,), (right_dim,)), ((), ())), preferred_element_type=F32
    )


def pack_kernel(q_ref, g_ref, out_ref):
    rows = q_ref.shape[0]
    out_ref[:rows] = q_ref[...]
    out_ref[rows:] = g_ref[...]


def stat_row(b, h, heads):
    return 2 * (b * heads + h)


def pair_terms(q, g, k, v, norm, delta, factor, keep):
    blank = jnp.zeros_like(q)
    queries = jnp.concatenate(
        [jnp.concatenate([q, blank], axis=1), jnp.concatenate([blank, g], axis=1)], axis=0
    )
    products = mm(jnp.concatenate([k, v], axis=1), queries, 1, 1)
    scores = products[:, :BLOCK] * factor
    weights = jnp.where(keep, jnp.exp(scores - norm), 0.0)
    dscores = weights * (products[:, BLOCK:] - delta)
    weights_b = weights.astype(BF16)
    dscores_b = dscores.astype(BF16)
    grads = mm(jnp.concatenate([dscores_b, weights_b], axis=1), queries, 1, 0)
    grad_q = mm(dscores_b, k, 0, 0) * factor
    return grad_q, grads[:, :BLOCK] * factor, grads[:, BLOCK:]


def own_kernel(
    blocks, heads, factor, q_ref, g_ref, o_ref, n_ref, k_ref, v_ref, stat_ref, dq_ref, dk_ref, dv_ref
):
    key_at = lax.broadcasted_iota(jnp.int32, (BLOCK, BLOCK), 0)
    query_at = lax.broadcasted_iota(jnp.int32, (BLOCK, BLOCK), 1)
    keep = key_at <= query_at
    for b in range(blocks):
        for h in range(heads):
            at = slice(b * BLOCK, (b + 1) * BLOCK)
            cols = slice(h * BLOCK, (h + 1) * BLOCK)
            product = g_ref[at, cols].astype(F32) * o_ref[at, cols].astype(F32)
            delta = jnp.sum(product.T, axis=0, keepdims=True)
            norm = n_ref[h : h + 1, at]
            row = stat_row(b, h, heads)
            stat_ref[row : row + 1] = norm
            stat_ref[row + 1 : row + 2] = delta
            grad_q, grad_k, grad_v = pair_terms(
                q_ref[at, cols], g_ref[at, cols], k_ref[at, cols], v_ref[at, cols], norm, delta, factor, keep
            )
            dq_ref[at, cols] = grad_q
            dk_ref[at, cols] = grad_k
            dv_ref[at, cols] = grad_v


def low_bits(value, size):
    return value & (size - 1), value >> (size.bit_length() - 1)


def remote_kernel(blocks, heads, factor, owners, *refs):
    slots_ref, stat_ref, own_q_ref, packs_ref, own_k_ref, own_v_ref = refs[:6]
    kv_refs = refs[6 : 6 + owners]
    dq_out, *part_outs = refs[6 + owners : 7 + 2 * owners]
    dq_ref, acc_ref, far_ref, line_ref, pack_ref, kv_ref, sems = refs[7 + 2 * owners :]
    rows = blocks * BLOCK
    span = blocks * owners
    loads = [
        pltpu.make_async_copy(packs_ref, pack_ref, sems.at[owners]),
        pltpu.make_async_copy(own_k_ref, acc_ref.at[0, pl.ds(0, rows)], sems.at[owners + 1]),
        pltpu.make_async_copy(own_v_ref, acc_ref.at[0, pl.ds(rows, rows)], sems.at[owners + 2]),
    ]
    for at in range(owners):
        loads.append(pltpu.make_async_copy(kv_refs[at], kv_ref.at[at], sems.at[at]))
    for load in loads:
        load.start()
    count = slots_ref[0]
    mine = slots_ref[slots_ref.shape[0] - 1]
    dq_ref[...] = jnp.zeros_like(dq_ref)
    dq_ref[mine] = own_q_ref[...].astype(BF16)
    acc_ref[1:] = jnp.zeros((owners - 1, *acc_ref.shape[1:]), F32)
    for load in loads:
        load.wait()

    def turn(step, carry):
        done = []
        for u in range(UNROLL):
            slot = step * UNROLL + u
            live = slot < count
            code = slots_ref[1 + jnp.where(live, slot, count - 1)]
            kb, rest = low_bits(code, blocks)
            kx, rest = low_bits(rest, owners)
            h, rest = low_bits(rest, heads)
            b, zq = low_bits(rest, blocks)
            cols = pl.ds(pl.multiple_of(h * BLOCK, BLOCK), BLOCK)
            q_at = pl.ds(pl.multiple_of(b * BLOCK, BLOCK), BLOCK)
            g_at = pl.ds(pl.multiple_of(rows + b * BLOCK, BLOCK), BLOCK)
            k_at = pl.ds(pl.multiple_of(kb * BLOCK, BLOCK), BLOCK)
            v_at = pl.ds(pl.multiple_of(rows + kb * BLOCK, BLOCK), BLOCK)
            row = stat_row(b, h, heads)
            norm = stat_ref[zq, pl.ds(row, 1), :]
            delta = stat_ref[zq, pl.ds(row + 1, 1), :]
            terms = pair_terms(
                pack_ref[zq, q_at, cols],
                pack_ref[zq, g_at, cols],
                kv_ref[kx, k_at, cols],
                kv_ref[kx, v_at, cols],
                norm,
                delta,
                factor,
                live,
            )
            before = slots_ref[jnp.where(live, slot, count)]
            shift = span.bit_length() - 1
            same = (slot > 0) & ((before >> shift) == (code >> shift))
            done.append((same, zq, q_at, cols, kx, k_at, v_at, terms))
        for same, zq, q_at, cols, kx, k_at, v_at, (grad_q, grad_k, grad_v) in done:
            acc_ref[kx, k_at, cols] += grad_k
            acc_ref[kx, v_at, cols] += grad_v
            start = jnp.where(zq == mine, own_q_ref[q_at, cols], 0.0)
            total = jnp.where(same, line_ref[...], start) + grad_q
            line_ref[...] = total
            dq_ref[zq, q_at, cols] = total.astype(BF16)
        return carry

    lax.fori_loop(0, (count + UNROLL - 1) // UNROLL, turn, 0)
    stores = [pltpu.make_async_copy(dq_ref, dq_out, sems.at[owners])]
    for at in range(PAIR):
        stores.append(pltpu.make_async_copy(acc_ref.at[at], part_outs[at], sems.at[at]))
    for store in stores:
        store.start()
    for at in range(PAIR, owners):
        far_ref[at - PAIR] = acc_ref[at].astype(BF16)
        turned = pltpu.make_async_copy(far_ref.at[at - PAIR], part_outs[at], sems.at[at])
        turned.start()
        stores.append(turned)
    for store in stores:
        store.wait()


def slot_codes(table, j, p, x, owners):
    ring, blocks, heads, top_count = table.shape
    slot_total = ring * owners * PER_PEER
    span = blocks * owners
    flat = table.reshape(-1)
    ids = jnp.arange(flat.shape[0], dtype=jnp.int32)
    hit = (flat >= 0) & (flat // span == j)
    owner = flat % span // blocks
    near = (owner % X_SIZE - x) % X_SIZE * PAIR + (owner // X_SIZE - p) % PAIR
    code = ids // top_count * span + near * blocks + flat % blocks
    earlier = (ids[None, :] <= ids[:, None]) & hit[None, :]
    place = jnp.sum(earlier.astype(jnp.int32), axis=1) - 1
    match = (place[None, :] == jnp.arange(slot_total, dtype=jnp.int32)[:, None]) & hit[None, :]
    codes = jnp.sum(jnp.where(match, code[None, :], 0), axis=1)
    return jnp.concatenate([jnp.sum(hit.astype(jnp.int32))[None], codes, j[None]])


def remote_call(codes, stats, own_q, packs, own_k, own_v, kvs, blocks, heads, factor, rows, width, ring, owners):
    anywhere = pl.BlockSpec(memory_space=pl.ANY)
    part = (2 * rows, width)
    return pl.pallas_call(
        functools.partial(remote_kernel, blocks, heads, factor, owners),
        in_specs=[pl.BlockSpec(memory_space=pltpu.SMEM)]
        + [pl.BlockSpec(memory_space=pltpu.VMEM)] * 2
        + [anywhere] * (3 + owners),
        out_specs=(anywhere,) * (1 + owners),
        out_shape=(jax.ShapeDtypeStruct((ring, rows, width), BF16),)
        + (jax.ShapeDtypeStruct(part, F32),) * PAIR
        + (jax.ShapeDtypeStruct(part, BF16),) * (owners - PAIR),
        scratch_shapes=[
            pltpu.VMEM((ring, rows, width), BF16),
            pltpu.VMEM((owners, *part), F32),
            pltpu.VMEM((owners - PAIR, *part), BF16),
            pltpu.VMEM((BLOCK, BLOCK), F32),
            pltpu.VMEM((ring, 2 * rows, width), BF16),
            pltpu.VMEM((owners, *part), BF16),
            pltpu.SemaphoreType.DMA((owners + 3,)),
        ],
        compiler_params=PARAMS,
        name="remote",
    )(codes, stats, own_q, packs, own_k, own_v, *kvs)


def shards(queries, keys, values, out_grad, outputs, log_norms, selected):
    blocks, heads, top_count = selected.shape
    rows, width = queries.shape
    factor = (width // heads) ** (-0.5)
    ring = lax.axis_size("j")
    owners = lax.axis_size("p") * lax.axis_size("x")
    pack = pl.pallas_call(
        pack_kernel,
        out_shape=jax.ShapeDtypeStruct((2 * rows, width), BF16),
        compiler_params=PARAMS,
        name="pack",
    )(queries, out_grad)
    packs = lax.all_gather(pack, "j")
    pack, selected, keys, values = lax.optimization_barrier((pack, selected, keys, values))
    both = jnp.concatenate([keys, values], axis=0)
    swapped = lax.ppermute(both, "p", [(i, (i + 1) % PAIR) for i in range(PAIR)])
    kvs = [both, swapped]
    for shift in range(1, X_SIZE):
        back = [(i, (i - shift) % X_SIZE) for i in range(X_SIZE)]
        kvs += [lax.ppermute(both, "x", back), lax.ppermute(swapped, "x", back)]
    own = jax.ShapeDtypeStruct((rows, width), F32)
    stats, own_q, own_k, own_v = pl.pallas_call(
        functools.partial(own_kernel, blocks, heads, factor),
        out_shape=(jax.ShapeDtypeStruct((2 * blocks * heads, BLOCK), F32), own, own, own),
        compiler_params=PARAMS,
        name="own",
    )(queries, out_grad, outputs, log_norms.T, keys, values)
    picks = jnp.pad(selected.reshape(-1).astype(F32), (0, BLOCK * 8 - selected.size))
    info = jnp.concatenate([stats, picks.reshape(8, BLOCK)], axis=0)
    stats = lax.all_to_all(jnp.broadcast_to(info[None], (ring, *info.shape)), "j", 0, 0, tiled=True)
    table = stats[:, 2 * blocks * heads, : selected.size].astype(jnp.int32)
    table = table.reshape(ring, *selected.shape)
    codes = slot_codes(table, lax.axis_index("j"), lax.axis_index("p"), lax.axis_index("x"), owners)
    packs, kvs, codes, stats, own_q, own_k, own_v = lax.optimization_barrier(
        (packs, kvs, codes, stats, own_q, own_k, own_v)
    )
    part_q, near, near_other, next_a, next_b, far_a, far_b, last_a, last_b = remote_call(
        codes, stats, own_q, packs, own_k, own_v, kvs, blocks, heads, factor, rows, width, ring, owners
    )
    sum_q = lax.psum_scatter(part_q, "j", scatter_dimension=0)
    ahead = [(i, (i + 1) % X_SIZE) for i in range(X_SIZE)]
    behind = [(i, (i - 1) % X_SIZE) for i in range(X_SIZE)]

    def wide(part):
        return part.astype(F32)

    through_a = lax.ppermute(far_a, "x", ahead)
    through_b = lax.ppermute(far_b, "x", behind)
    from_next = lax.ppermute(next_b, "x", ahead)
    from_last = lax.ppermute(last_a, "x", behind)
    next_a = (wide(next_a) + wide(through_a)).astype(BF16)
    last_b = (wide(last_b) + wide(through_b)).astype(BF16)
    sum_own = near + wide(from_last) + wide(lax.ppermute(next_a, "x", ahead))
    sum_other = near_other + wide(from_next) + wide(lax.ppermute(last_b, "x", behind))
    sum_other, sum_own, sum_q = lax.optimization_barrier((sum_other.astype(BF16), sum_own, sum_q))
    crossed = lax.ppermute(sum_other, "p", [(i, (i + 1) % PAIR) for i in range(PAIR)])
    final_kv = sum_own + wide(crossed)
    final_k = final_kv[:rows].astype(BF16)
    final_v = final_kv[rows:].astype(BF16)
    spread_q = lax.all_to_all(sum_q, "head", split_axis=0, concat_axis=1, tiled=True)
    return spread_q, final_k, final_v


def solution(mesh):
    ctx_count, head_count = mesh.devices.shape
    grid = mesh.devices.reshape(ctx_count // (PAIR * X_SIZE), PAIR, X_SIZE, head_count)
    fine = Mesh(grid, ("j", "p", "x", "head"))
    ctx = ("j", "p", "x")
    placed = P(ctx, "head")
    return jax.shard_map(
        shards,
        mesh=fine,
        in_specs=(placed,) * 6 + (P(ctx, "head", None),),
        out_specs=(P((*ctx, "head"), None), placed, placed),
        check_vma=False,
    )
```

```python
import functools

import jax
import jax.numpy as jnp
from jax import lax
from jax.experimental import pallas as pl
from jax.experimental.pallas import tpu as pltpu
from jax.sharding import Mesh
from jax.sharding import PartitionSpec as P

X_SIZE = 4
BLOCK = 128
PER_PEER = 2
PAIR = 2
UNROLL = 8
F32 = jnp.float32
BF16 = jnp.bfloat16
PARAMS = pltpu.CompilerParams(vmem_limit_bytes=56 * 1024 * 1024)


def mm(left, right, left_dim, right_dim):
    return lax.dot_general(
        left, right, (((left_dim,), (right_dim,)), ((), ())), preferred_element_type=F32
    )


def pack_kernel(q_ref, g_ref, out_ref):
    rows = q_ref.shape[0]
    out_ref[:rows] = q_ref[...]
    out_ref[rows:] = g_ref[...]


def stat_row(b, h, heads):
    return 2 * (b * heads + h)


def pair_terms(q, g, k, v, norm, delta, factor, keep):
    blank = jnp.zeros_like(q)
    queries = jnp.concatenate(
        [jnp.concatenate([q, blank], axis=1), jnp.concatenate([blank, g], axis=1)], axis=0
    )
    products = mm(jnp.concatenate([k, v], axis=1), queries, 1, 1)
    scores = products[:, :BLOCK] * factor
    weights = jnp.where(keep, jnp.exp(scores - norm), 0.0)
    dscores = weights * (products[:, BLOCK:] - delta)
    weights_b = weights.astype(BF16)
    dscores_b = dscores.astype(BF16)
    grads = mm(jnp.concatenate([dscores_b, weights_b], axis=1), queries, 1, 0)
    grad_q = mm(dscores_b, k, 0, 0) * factor
    return grad_q, grads[:, :BLOCK] * factor, grads[:, BLOCK:]


def own_kernel(
    blocks, heads, factor, q_ref, g_ref, o_ref, n_ref, k_ref, v_ref, stat_ref, dq_ref, dk_ref, dv_ref
):
    key_at = lax.broadcasted_iota(jnp.int32, (BLOCK, BLOCK), 0)
    query_at = lax.broadcasted_iota(jnp.int32, (BLOCK, BLOCK), 1)
    keep = key_at <= query_at
    for b in range(blocks):
        for h in range(heads):
            at = slice(b * BLOCK, (b + 1) * BLOCK)
            cols = slice(h * BLOCK, (h + 1) * BLOCK)
            product = g_ref[at, cols].astype(F32) * o_ref[at, cols].astype(F32)
            delta = jnp.sum(product.T, axis=0, keepdims=True)
            norm = n_ref[h : h + 1, at]
            row = stat_row(b, h, heads)
            stat_ref[row : row + 1] = norm
            stat_ref[row + 1 : row + 2] = delta
            grad_q, grad_k, grad_v = pair_terms(
                q_ref[at, cols], g_ref[at, cols], k_ref[at, cols], v_ref[at, cols], norm, delta, factor, keep
            )
            dq_ref[at, cols] = grad_q
            dk_ref[at, cols] = grad_k
            dv_ref[at, cols] = grad_v


def low_bits(value, size):
    return value & (size - 1), value >> (size.bit_length() - 1)


def remote_kernel(blocks, heads, factor, owners, *refs):
    slots_ref, stat_ref, own_q_ref, packs_ref, own_k_ref, own_v_ref = refs[:6]
    kv_refs = refs[6 : 6 + owners]
    dq_out, *part_outs = refs[6 + owners : 7 + 2 * owners]
    dq_ref, acc_ref, far_ref, line_ref, pack_ref, kv_ref, sems = refs[7 + 2 * owners :]
    rows = blocks * BLOCK
    span = blocks * owners
    loads = [
        pltpu.make_async_copy(packs_ref, pack_ref, sems.at[owners]),
        pltpu.make_async_copy(own_k_ref, acc_ref.at[0, pl.ds(0, rows)], sems.at[owners + 1]),
        pltpu.make_async_copy(own_v_ref, acc_ref.at[0, pl.ds(rows, rows)], sems.at[owners + 2]),
    ]
    for at in range(owners):
        loads.append(pltpu.make_async_copy(kv_refs[at], kv_ref.at[at], sems.at[at]))
    for load in loads:
        load.start()
    count = slots_ref[0]
    mine = slots_ref[slots_ref.shape[0] - 1]
    dq_ref[...] = jnp.zeros_like(dq_ref)
    dq_ref[mine] = own_q_ref[...].astype(BF16)
    acc_ref[1:] = jnp.zeros((owners - 1, *acc_ref.shape[1:]), F32)
    for load in loads:
        load.wait()

    def turn(step, carry):
        done = []
        for u in range(UNROLL):
            slot = step * UNROLL + u
            live = slot < count
            code = slots_ref[1 + jnp.where(live, slot, count - 1)]
            kb, rest = low_bits(code, blocks)
            kx, rest = low_bits(rest, owners)
            h, rest = low_bits(rest, heads)
            b, zq = low_bits(rest, blocks)
            cols = pl.ds(pl.multiple_of(h * BLOCK, BLOCK), BLOCK)
            q_at = pl.ds(pl.multiple_of(b * BLOCK, BLOCK), BLOCK)
            g_at = pl.ds(pl.multiple_of(rows + b * BLOCK, BLOCK), BLOCK)
            k_at = pl.ds(pl.multiple_of(kb * BLOCK, BLOCK), BLOCK)
            v_at = pl.ds(pl.multiple_of(rows + kb * BLOCK, BLOCK), BLOCK)
            row = stat_row(b, h, heads)
            norm = stat_ref[zq, pl.ds(row, 1), :]
            delta = stat_ref[zq, pl.ds(row + 1, 1), :]
            terms = pair_terms(
                pack_ref[zq, q_at, cols],
                pack_ref[zq, g_at, cols],
                kv_ref[kx, k_at, cols],
                kv_ref[kx, v_at, cols],
                norm,
                delta,
                factor,
                live,
            )
            before = slots_ref[jnp.where(live, slot, count)]
            shift = span.bit_length() - 1
            same = (slot > 0) & ((before >> shift) == (code >> shift))
            done.append((same, zq, q_at, cols, kx, k_at, v_at, terms))
        for same, zq, q_at, cols, kx, k_at, v_at, (grad_q, grad_k, grad_v) in done:
            acc_ref[kx, k_at, cols] += grad_k
            acc_ref[kx, v_at, cols] += grad_v
            start = jnp.where(zq == mine, own_q_ref[q_at, cols], 0.0)
            total = jnp.where(same, line_ref[...], start) + grad_q
            line_ref[...] = total
            dq_ref[zq, q_at, cols] = total.astype(BF16)
        return carry

    lax.fori_loop(0, (count + UNROLL - 1) // UNROLL, turn, 0)
    stores = [pltpu.make_async_copy(dq_ref, dq_out, sems.at[owners])]
    for at in range(PAIR):
        stores.append(pltpu.make_async_copy(acc_ref.at[at], part_outs[at], sems.at[at]))
    for store in stores:
        store.start()
    for at in range(PAIR, owners):
        far_ref[at - PAIR] = acc_ref[at].astype(BF16)
        turned = pltpu.make_async_copy(far_ref.at[at - PAIR], part_outs[at], sems.at[at])
        turned.start()
        stores.append(turned)
    for store in stores:
        store.wait()


def slot_codes(table, j, p, x, owners):
    ring, blocks, heads, top_count = table.shape
    slot_total = ring * owners * PER_PEER
    span = blocks * owners
    flat = table.reshape(-1)
    ids = jnp.arange(flat.shape[0], dtype=jnp.int32)
    hit = (flat >= 0) & (flat // span == j)
    owner = flat % span // blocks
    near = (owner % X_SIZE - x) % X_SIZE * PAIR + (owner // X_SIZE - p) % PAIR
    code = ids // top_count * span + near * blocks + flat % blocks
    earlier = (ids[None, :] <= ids[:, None]) & hit[None, :]
    place = jnp.sum(earlier.astype(jnp.int32), axis=1) - 1
    match = (place[None, :] == jnp.arange(slot_total, dtype=jnp.int32)[:, None]) & hit[None, :]
    codes = jnp.sum(jnp.where(match, code[None, :], 0), axis=1)
    return jnp.concatenate([jnp.sum(hit.astype(jnp.int32))[None], codes, j[None]])


def remote_call(codes, stats, own_q, packs, own_k, own_v, kvs, blocks, heads, factor, rows, width, ring, owners):
    anywhere = pl.BlockSpec(memory_space=pl.ANY)
    part = (2 * rows, width)
    return pl.pallas_call(
        functools.partial(remote_kernel, blocks, heads, factor, owners),
        in_specs=[pl.BlockSpec(memory_space=pltpu.SMEM)]
        + [pl.BlockSpec(memory_space=pltpu.VMEM)] * 2
        + [anywhere] * (3 + owners),
        out_specs=(anywhere,) * (1 + owners),
        out_shape=(jax.ShapeDtypeStruct((ring, rows, width), BF16),)
        + (jax.ShapeDtypeStruct(part, F32),) * PAIR
        + (jax.ShapeDtypeStruct(part, BF16),) * (owners - PAIR),
        scratch_shapes=[
            pltpu.VMEM((ring, rows, width), BF16),
            pltpu.VMEM((owners, *part), F32),
            pltpu.VMEM((owners - PAIR, *part), BF16),
            pltpu.VMEM((BLOCK, BLOCK), F32),
            pltpu.VMEM((ring, 2 * rows, width), BF16),
            pltpu.VMEM((owners, *part), BF16),
            pltpu.SemaphoreType.DMA((owners + 3,)),
        ],
        compiler_params=PARAMS,
        name="remote",
    )(codes, stats, own_q, packs, own_k, own_v, *kvs)


def shards(queries, keys, values, out_grad, outputs, log_norms, selected):
    blocks, heads, top_count = selected.shape
    rows, width = queries.shape
    factor = (width // heads) ** (-0.5)
    ring = lax.axis_size("j")
    owners = lax.axis_size("p") * lax.axis_size("x")
    pack = pl.pallas_call(
        pack_kernel,
        out_shape=jax.ShapeDtypeStruct((2 * rows, width), BF16),
        compiler_params=PARAMS,
        name="pack",
    )(queries, out_grad)
    packs = lax.all_gather(pack, "j")
    pack, selected, keys, values = lax.optimization_barrier((pack, selected, keys, values))
    both = jnp.concatenate([keys, values], axis=0)
    swapped = lax.ppermute(both, "p", [(i, (i + 1) % PAIR) for i in range(PAIR)])
    kvs = [both, swapped]
    for shift in range(1, X_SIZE):
        back = [(i, (i - shift) % X_SIZE) for i in range(X_SIZE)]
        kvs += [lax.ppermute(both, "x", back), lax.ppermute(swapped, "x", back)]
    own = jax.ShapeDtypeStruct((rows, width), F32)
    stats, own_q, own_k, own_v = pl.pallas_call(
        functools.partial(own_kernel, blocks, heads, factor),
        out_shape=(jax.ShapeDtypeStruct((2 * blocks * heads, BLOCK), F32), own, own, own),
        compiler_params=PARAMS,
        name="own",
    )(queries, out_grad, outputs, log_norms.T, keys, values)
    stats, selected, swapped = lax.optimization_barrier((stats, selected, swapped))
    picks = jnp.pad(selected.reshape(-1).astype(F32), (0, BLOCK * 8 - selected.size))
    info = jnp.concatenate([stats, picks.reshape(8, BLOCK)], axis=0)
    stats = lax.all_to_all(jnp.broadcast_to(info[None], (ring, *info.shape)), "j", 0, 0, tiled=True)
    table = stats[:, 2 * blocks * heads, : selected.size].astype(jnp.int32)
    table = table.reshape(ring, *selected.shape)
    codes = slot_codes(table, lax.axis_index("j"), lax.axis_index("p"), lax.axis_index("x"), owners)
    packs, kvs, codes, stats, own_q, own_k, own_v = lax.optimization_barrier(
        (packs, kvs, codes, stats, own_q, own_k, own_v)
    )
    part_q, near, near_other, next_a, next_b, far_a, far_b, last_a, last_b = remote_call(
        codes, stats, own_q, packs, own_k, own_v, kvs, blocks, heads, factor, rows, width, ring, owners
    )
    sum_q = lax.psum_scatter(part_q, "j", scatter_dimension=0)
    ahead = [(i, (i + 1) % X_SIZE) for i in range(X_SIZE)]
    behind = [(i, (i - 1) % X_SIZE) for i in range(X_SIZE)]

    def wide(part):
        return part.astype(F32)

    through_a = lax.ppermute(far_a, "x", ahead)
    through_b = lax.ppermute(far_b, "x", behind)
    from_next = lax.ppermute(next_b, "x", ahead)
    from_last = lax.ppermute(last_a, "x", behind)
    next_a = (wide(next_a) + wide(through_a)).astype(BF16)
    last_b = (wide(last_b) + wide(through_b)).astype(BF16)
    sum_own = near + wide(from_last) + wide(lax.ppermute(next_a, "x", ahead))
    sum_other = near_other + wide(from_next) + wide(lax.ppermute(last_b, "x", behind))
    sum_other, sum_own, sum_q = lax.optimization_barrier((sum_other.astype(BF16), sum_own, sum_q))
    crossed = lax.ppermute(sum_other, "p", [(i, (i + 1) % PAIR) for i in range(PAIR)])
    final_kv = sum_own + wide(crossed)
    final_k = final_kv[:rows].astype(BF16)
    final_v = final_kv[rows:].astype(BF16)
    spread_q = lax.all_to_all(sum_q, "head", split_axis=0, concat_axis=1, tiled=True)
    return spread_q, final_k, final_v


def solution(mesh):
    ctx_count, head_count = mesh.devices.shape
    grid = mesh.devices.reshape(ctx_count // (PAIR * X_SIZE), PAIR, X_SIZE, head_count)
    fine = Mesh(grid, ("j", "p", "x", "head"))
    ctx = ("j", "p", "x")
    placed = P(ctx, "head")
    return jax.shard_map(
        shards,
        mesh=fine,
        in_specs=(placed,) * 6 + (P(ctx, "head", None),),
        out_specs=(P((*ctx, "head"), None), placed, placed),
        check_vma=False,
    )
```

```python
import functools

import jax
import jax.numpy as jnp
from jax import lax
from jax.experimental import pallas as pl
from jax.experimental.pallas import tpu as pltpu
from jax.sharding import Mesh
from jax.sharding import PartitionSpec as P

X_SIZE = 4
BLOCK = 128
PER_PEER = 2
PAIR = 2
TURN_SIZES = (16, 4)
F32 = jnp.float32
BF16 = jnp.bfloat16
PARAMS = pltpu.CompilerParams(vmem_limit_bytes=56 * 1024 * 1024)


def mm(left, right, left_dim, right_dim):
    return lax.dot_general(
        left, right, (((left_dim,), (right_dim,)), ((), ())), preferred_element_type=F32
    )


def pack_kernel(q_ref, g_ref, out_ref):
    rows = q_ref.shape[0]
    out_ref[:rows] = q_ref[...]
    out_ref[rows:] = g_ref[...]


def stat_row(b, h, heads):
    return 2 * (b * heads + h)


def pair_terms(q, g, k, v, norm, delta, factor, keep):
    blank = jnp.zeros_like(q)
    queries = jnp.concatenate(
        [jnp.concatenate([q, blank], axis=1), jnp.concatenate([blank, g], axis=1)], axis=0
    )
    products = mm(jnp.concatenate([k, v], axis=1), queries, 1, 1)
    scores = products[:, :BLOCK] * factor
    weights = jnp.where(keep, jnp.exp(scores - norm), 0.0)
    dscores = weights * (products[:, BLOCK:] - delta)
    weights_b = weights.astype(BF16)
    dscores_b = dscores.astype(BF16)
    grads = mm(jnp.concatenate([dscores_b, weights_b], axis=1), queries, 1, 0)
    grad_q = mm(dscores_b, k, 0, 0) * factor
    return grad_q, grads[:, :BLOCK] * factor, grads[:, BLOCK:]


def own_kernel(
    blocks, heads, factor, q_ref, g_ref, o_ref, n_ref, k_ref, v_ref, stat_ref, dq_ref, dk_ref, dv_ref
):
    key_at = lax.broadcasted_iota(jnp.int32, (BLOCK, BLOCK), 0)
    query_at = lax.broadcasted_iota(jnp.int32, (BLOCK, BLOCK), 1)
    keep = key_at <= query_at
    for b in range(blocks):
        for h in range(heads):
            at = slice(b * BLOCK, (b + 1) * BLOCK)
            cols = slice(h * BLOCK, (h + 1) * BLOCK)
            product = g_ref[at, cols].astype(F32) * o_ref[at, cols].astype(F32)
            delta = jnp.sum(product.T, axis=0, keepdims=True)
            norm = n_ref[h : h + 1, at]
            row = stat_row(b, h, heads)
            stat_ref[row : row + 1] = norm
            stat_ref[row + 1 : row + 2] = delta
            grad_q, grad_k, grad_v = pair_terms(
                q_ref[at, cols], g_ref[at, cols], k_ref[at, cols], v_ref[at, cols], norm, delta, factor, keep
            )
            dq_ref[at, cols] = grad_q
            dk_ref[at, cols] = grad_k
            dv_ref[at, cols] = grad_v


def low_bits(value, size):
    return value & (size - 1), value >> (size.bit_length() - 1)


def remote_kernel(blocks, heads, factor, owners, *refs):
    slots_ref, stat_ref, own_q_ref, own_k_ref, own_v_ref, packs_ref = refs[:6]
    kv_refs = refs[6 : 6 + owners]
    dq_out, *part_outs = refs[6 + owners : 7 + 2 * owners]
    dq_ref, acc_ref, far_ref, line_ref, pack_ref, kv_ref, sems = refs[7 + 2 * owners :]
    rows = blocks * BLOCK
    span = blocks * owners
    loads = [
        pltpu.make_async_copy(packs_ref, pack_ref, sems.at[owners]),
    ]
    for at in range(owners):
        loads.append(pltpu.make_async_copy(kv_refs[at], kv_ref.at[at], sems.at[at]))
    for load in loads:
        load.start()
    count = slots_ref[0]
    mine = slots_ref[slots_ref.shape[0] - 1]
    dq_ref[...] = jnp.zeros_like(dq_ref)
    dq_ref[mine] = own_q_ref[...].astype(BF16)
    acc_ref[0, :rows] = own_k_ref[...]
    acc_ref[0, rows:] = own_v_ref[...]
    acc_ref[1:] = jnp.zeros((owners - 1, *acc_ref.shape[1:]), F32)
    for load in loads:
        load.wait()

    def turn(first, size):
        done = []
        for u in range(size):
            slot = first + u
            live = slot < count
            code = slots_ref[1 + jnp.where(live, slot, count - 1)]
            kb, rest = low_bits(code, blocks)
            kx, rest = low_bits(rest, owners)
            h, rest = low_bits(rest, heads)
            b, zq = low_bits(rest, blocks)
            cols = pl.ds(pl.multiple_of(h * BLOCK, BLOCK), BLOCK)
            q_at = pl.ds(pl.multiple_of(b * BLOCK, BLOCK), BLOCK)
            g_at = pl.ds(pl.multiple_of(rows + b * BLOCK, BLOCK), BLOCK)
            k_at = pl.ds(pl.multiple_of(kb * BLOCK, BLOCK), BLOCK)
            v_at = pl.ds(pl.multiple_of(rows + kb * BLOCK, BLOCK), BLOCK)
            row = stat_row(b, h, heads)
            norm = stat_ref[zq, pl.ds(row, 1), :]
            delta = stat_ref[zq, pl.ds(row + 1, 1), :]
            terms = pair_terms(
                pack_ref[zq, q_at, cols],
                pack_ref[zq, g_at, cols],
                kv_ref[kx, k_at, cols],
                kv_ref[kx, v_at, cols],
                norm,
                delta,
                factor,
                live,
            )
            before = slots_ref[jnp.where(live, slot, count)]
            shift = span.bit_length() - 1
            same = (slot > 0) & ((before >> shift) == (code >> shift))
            done.append((same, zq, q_at, cols, kx, k_at, v_at, terms))
        for same, zq, q_at, cols, kx, k_at, v_at, (grad_q, grad_k, grad_v) in done:
            acc_ref[kx, k_at, cols] += grad_k
            acc_ref[kx, v_at, cols] += grad_v
            start = jnp.where(zq == mine, own_q_ref[q_at, cols], 0.0)
            total = jnp.where(same, line_ref[...], start) + grad_q
            line_ref[...] = total
            dq_ref[zq, q_at, cols] = total.astype(BF16)

    large, small = TURN_SIZES
    full, rest = low_bits(count, large)[::-1]

    @pl.loop(0, full)
    def _(step):
        turn(step * large, large)

    @pl.loop(0, low_bits(rest + small - 1, small)[1])
    def _(step):
        turn(full * large + step * small, small)

    stores = [pltpu.make_async_copy(dq_ref, dq_out, sems.at[owners])]
    for at in range(PAIR):
        stores.append(pltpu.make_async_copy(acc_ref.at[at], part_outs[at], sems.at[at]))
    for store in stores:
        store.start()
    for at in range(PAIR, owners):
        far_ref[at - PAIR] = acc_ref[at].astype(BF16)
        turned = pltpu.make_async_copy(far_ref.at[at - PAIR], part_outs[at], sems.at[at])
        turned.start()
        stores.append(turned)
    for store in stores:
        store.wait()


def slot_codes(table, j, p, x, owners):
    ring, blocks, heads, top_count = table.shape
    slot_total = ring * owners * PER_PEER
    span = blocks * owners
    flat = table.reshape(-1)
    ids = jnp.arange(flat.shape[0], dtype=jnp.int32)
    hit = (flat >= 0) & (flat // span == j)
    owner = flat % span // blocks
    near = (owner % X_SIZE - x) % X_SIZE * PAIR + (owner // X_SIZE - p) % PAIR
    code = ids // top_count * span + near * blocks + flat % blocks
    earlier = (ids[None, :] <= ids[:, None]) & hit[None, :]
    place = jnp.sum(earlier.astype(jnp.int32), axis=1) - 1
    match = (place[None, :] == jnp.arange(slot_total, dtype=jnp.int32)[:, None]) & hit[None, :]
    codes = jnp.sum(jnp.where(match, code[None, :], 0), axis=1)
    return jnp.concatenate([jnp.sum(hit.astype(jnp.int32))[None], codes, j[None]])


def remote_call(codes, stats, own_q, packs, own_k, own_v, kvs, blocks, heads, factor, rows, width, ring, owners):
    anywhere = pl.BlockSpec(memory_space=pl.ANY)
    part = (2 * rows, width)
    return pl.pallas_call(
        functools.partial(remote_kernel, blocks, heads, factor, owners),
        in_specs=[pl.BlockSpec(memory_space=pltpu.SMEM)]
        + [pl.BlockSpec(memory_space=pltpu.VMEM)] * 4
        + [anywhere] * (1 + owners),
        out_specs=(anywhere,) * (1 + owners),
        out_shape=(jax.ShapeDtypeStruct((ring, rows, width), BF16),)
        + (jax.ShapeDtypeStruct(part, F32),) * PAIR
        + (jax.ShapeDtypeStruct(part, BF16),) * (owners - PAIR),
        scratch_shapes=[
            pltpu.VMEM((ring, rows, width), BF16),
            pltpu.VMEM((owners, *part), F32),
            pltpu.VMEM((owners - PAIR, *part), BF16),
            pltpu.VMEM((BLOCK, BLOCK), F32),
            pltpu.VMEM((ring, 2 * rows, width), BF16),
            pltpu.VMEM((owners, *part), BF16),
            pltpu.SemaphoreType.DMA((owners + 1,)),
        ],
        compiler_params=PARAMS,
        name="remote",
    )(codes, stats, own_q, own_k, own_v, packs, *kvs)


def shards(queries, keys, values, out_grad, outputs, log_norms, selected):
    blocks, heads, top_count = selected.shape
    rows, width = queries.shape
    factor = (width // heads) ** (-0.5)
    ring = lax.axis_size("j")
    owners = lax.axis_size("p") * lax.axis_size("x")
    pack = pl.pallas_call(
        pack_kernel,
        out_shape=jax.ShapeDtypeStruct((2 * rows, width), BF16),
        compiler_params=PARAMS,
        name="pack",
    )(queries, out_grad)
    packs = lax.all_gather(pack, "j")
    pack, selected, keys, values = lax.optimization_barrier((pack, selected, keys, values))
    both = jnp.concatenate([keys, values], axis=0)
    swapped = lax.ppermute(both, "p", [(i, (i + 1) % PAIR) for i in range(PAIR)])
    kvs = [both, swapped]
    for shift in range(1, X_SIZE):
        back = [(i, (i - shift) % X_SIZE) for i in range(X_SIZE)]
        kvs += [lax.ppermute(both, "x", back), lax.ppermute(swapped, "x", back)]
    own = jax.ShapeDtypeStruct((rows, width), F32)
    stats, own_q, own_k, own_v = pl.pallas_call(
        functools.partial(own_kernel, blocks, heads, factor),
        out_shape=(jax.ShapeDtypeStruct((2 * blocks * heads, BLOCK), F32), own, own, own),
        compiler_params=PARAMS,
        name="own",
    )(queries, out_grad, outputs, log_norms.T, keys, values)
    stats, selected, swapped = lax.optimization_barrier((stats, selected, swapped))
    picks = jnp.pad(selected.reshape(-1).astype(F32), (0, BLOCK * 8 - selected.size))
    info = jnp.concatenate([stats, picks.reshape(8, BLOCK)], axis=0)
    stats = lax.all_to_all(jnp.broadcast_to(info[None], (ring, *info.shape)), "j", 0, 0, tiled=True)
    table = stats[:, 2 * blocks * heads, : selected.size].astype(jnp.int32)
    table = table.reshape(ring, *selected.shape)
    codes = slot_codes(table, lax.axis_index("j"), lax.axis_index("p"), lax.axis_index("x"), owners)
    packs, kvs, codes, stats, own_q, own_k, own_v = lax.optimization_barrier(
        (packs, kvs, codes, stats, own_q, own_k, own_v)
    )
    part_q, near, near_other, next_a, next_b, far_a, far_b, last_a, last_b = remote_call(
        codes, stats, own_q, packs, own_k, own_v, kvs, blocks, heads, factor, rows, width, ring, owners
    )
    sum_q = lax.psum_scatter(part_q, "j", scatter_dimension=0)
    ahead = [(i, (i + 1) % X_SIZE) for i in range(X_SIZE)]
    behind = [(i, (i - 1) % X_SIZE) for i in range(X_SIZE)]

    def wide(part):
        return part.astype(F32)

    through_a = lax.ppermute(far_a, "x", ahead)
    through_b = lax.ppermute(far_b, "x", behind)
    from_next = lax.ppermute(next_b, "x", ahead)
    from_last = lax.ppermute(last_a, "x", behind)
    next_a = (wide(next_a) + wide(through_a)).astype(BF16)
    last_b = (wide(last_b) + wide(through_b)).astype(BF16)
    sum_own = near + wide(from_last) + wide(lax.ppermute(next_a, "x", ahead))
    sum_other = near_other + wide(from_next) + wide(lax.ppermute(last_b, "x", behind))
    sum_other, sum_own, sum_q = lax.optimization_barrier((sum_other.astype(BF16), sum_own, sum_q))
    crossed = lax.ppermute(sum_other, "p", [(i, (i + 1) % PAIR) for i in range(PAIR)])
    final_kv = sum_own + wide(crossed)
    final_k = final_kv[:rows].astype(BF16)
    final_v = final_kv[rows:].astype(BF16)
    spread_q = lax.all_to_all(sum_q, "head", split_axis=0, concat_axis=1, tiled=True)
    return spread_q, final_k, final_v


def solution(mesh):
    ctx_count, head_count = mesh.devices.shape
    grid = mesh.devices.reshape(ctx_count // (PAIR * X_SIZE), PAIR, X_SIZE, head_count)
    fine = Mesh(grid, ("j", "p", "x", "head"))
    ctx = ("j", "p", "x")
    placed = P(ctx, "head")
    return jax.shard_map(
        shards,
        mesh=fine,
        in_specs=(placed,) * 6 + (P(ctx, "head", None),),
        out_specs=(P((*ctx, "head"), None), placed, placed),
        check_vma=False,
    )
```

```python
import functools

import jax
import jax.numpy as jnp
from jax import lax
from jax.experimental import pallas as pl
from jax.experimental.pallas import tpu as pltpu
from jax.sharding import Mesh
from jax.sharding import PartitionSpec as P

X_SIZE = 4
BLOCK = 128
PER_PEER = 2
PAIR = 2
TURN_SIZES = (16, 4)
F32 = jnp.float32
BF16 = jnp.bfloat16
PARAMS = pltpu.CompilerParams(vmem_limit_bytes=56 * 1024 * 1024)


def mm(left, right, left_dim, right_dim):
    return lax.dot_general(
        left, right, (((left_dim,), (right_dim,)), ((), ())), preferred_element_type=F32
    )


def pack_kernel(q_ref, g_ref, out_ref):
    rows = q_ref.shape[0]
    out_ref[:rows] = q_ref[...]
    out_ref[rows:] = g_ref[...]


def stat_row(b, h, heads):
    return 2 * (b * heads + h)


def pair_terms(q, g, k, v, norm, delta, factor, keep):
    blank = jnp.zeros_like(q)
    queries = jnp.concatenate(
        [jnp.concatenate([q, blank], axis=1), jnp.concatenate([blank, g], axis=1)], axis=0
    )
    products = mm(jnp.concatenate([k, v], axis=1), queries, 1, 1)
    scores = products[:, :BLOCK] * factor
    weights = jnp.where(keep, jnp.exp(scores - norm), 0.0)
    dscores = weights * (products[:, BLOCK:] - delta)
    weights_b = weights.astype(BF16)
    dscores_b = dscores.astype(BF16)
    grads = mm(jnp.concatenate([dscores_b, weights_b], axis=1), queries, 1, 0)
    grad_q = mm(dscores_b, k, 0, 0) * factor
    return grad_q, grads[:, :BLOCK] * factor, grads[:, BLOCK:]


def own_kernel(
    blocks, heads, factor, q_ref, g_ref, o_ref, n_ref, k_ref, v_ref, stat_ref, dq_ref, dk_ref, dv_ref
):
    key_at = lax.broadcasted_iota(jnp.int32, (BLOCK, BLOCK), 0)
    query_at = lax.broadcasted_iota(jnp.int32, (BLOCK, BLOCK), 1)
    keep = key_at <= query_at
    for b in range(blocks):
        for h in range(heads):
            at = slice(b * BLOCK, (b + 1) * BLOCK)
            cols = slice(h * BLOCK, (h + 1) * BLOCK)
            product = g_ref[at, cols].astype(F32) * o_ref[at, cols].astype(F32)
            delta = jnp.sum(product.T, axis=0, keepdims=True)
            norm = n_ref[h : h + 1, at]
            row = stat_row(b, h, heads)
            stat_ref[row : row + 1] = norm
            stat_ref[row + 1 : row + 2] = delta
            grad_q, grad_k, grad_v = pair_terms(
                q_ref[at, cols], g_ref[at, cols], k_ref[at, cols], v_ref[at, cols], norm, delta, factor, keep
            )
            dq_ref[at, cols] = grad_q
            dk_ref[at, cols] = grad_k
            dv_ref[at, cols] = grad_v


def low_bits(value, size):
    return value & (size - 1), value >> (size.bit_length() - 1)


def remote_kernel(blocks, heads, factor, owners, *refs):
    slots_ref, stat_ref, own_q_ref, own_k_ref, own_v_ref, packs_ref = refs[:6]
    kv_refs = refs[6 : 6 + owners]
    ring = packs_ref.shape[0]
    outs = refs[6 + owners : -7]
    dq_outs, part_outs = outs[: ring + 1], outs[ring + 1 :]
    dq_ref, acc_ref, far_ref, line_ref, pack_ref, kv_ref, sems = refs[-7:]
    rows = blocks * BLOCK
    span = blocks * owners
    loads = [
        pltpu.make_async_copy(packs_ref, pack_ref, sems.at[owners]),
    ]
    for at in range(owners):
        loads.append(pltpu.make_async_copy(kv_refs[at], kv_ref.at[at], sems.at[at]))
    for load in loads:
        load.start()
    count = slots_ref[0]
    mine = slots_ref[slots_ref.shape[0] - 1]
    dq_ref[...] = jnp.zeros_like(dq_ref)
    acc_ref[0, :rows] = own_k_ref[...]
    acc_ref[0, rows:] = own_v_ref[...]
    acc_ref[1:] = jnp.zeros((owners - 1, *acc_ref.shape[1:]), F32)
    for load in loads:
        load.wait()

    def turn(first, size):
        done = []
        for u in range(size):
            slot = first + u
            live = slot < count
            code = slots_ref[1 + jnp.where(live, slot, count - 1)]
            kb, rest = low_bits(code, blocks)
            kx, rest = low_bits(rest, owners)
            h, rest = low_bits(rest, heads)
            b, zq = low_bits(rest, blocks)
            cols = pl.ds(pl.multiple_of(h * BLOCK, BLOCK), BLOCK)
            q_at = pl.ds(pl.multiple_of(b * BLOCK, BLOCK), BLOCK)
            g_at = pl.ds(pl.multiple_of(rows + b * BLOCK, BLOCK), BLOCK)
            k_at = pl.ds(pl.multiple_of(kb * BLOCK, BLOCK), BLOCK)
            v_at = pl.ds(pl.multiple_of(rows + kb * BLOCK, BLOCK), BLOCK)
            row = stat_row(b, h, heads)
            norm = stat_ref[zq, pl.ds(row, 1), :]
            delta = stat_ref[zq, pl.ds(row + 1, 1), :]
            terms = pair_terms(
                pack_ref[zq, q_at, cols],
                pack_ref[zq, g_at, cols],
                kv_ref[kx, k_at, cols],
                kv_ref[kx, v_at, cols],
                norm,
                delta,
                factor,
                live,
            )
            before = slots_ref[jnp.where(live, slot, count)]
            shift = span.bit_length() - 1
            same = (slot > 0) & ((before >> shift) == (code >> shift))
            done.append((same, zq, q_at, cols, kx, k_at, v_at, terms))
        for same, zq, q_at, cols, kx, k_at, v_at, (grad_q, grad_k, grad_v) in done:
            acc_ref[kx, k_at, cols] += grad_k
            acc_ref[kx, v_at, cols] += grad_v
            total = jnp.where(same, line_ref[...], 0.0) + grad_q
            line_ref[...] = total
            dq_ref[(zq - mine) & (ring - 1), q_at, cols] = total

    large, small = TURN_SIZES
    full, rest = low_bits(count, large)[::-1]

    @pl.loop(0, full)
    def _(step):
        turn(step * large, large)

    @pl.loop(0, low_bits(rest + small - 1, small)[1])
    def _(step):
        turn(full * large + step * small, small)

    stores = []
    for at in range(PAIR):
        stores.append(pltpu.make_async_copy(acc_ref.at[at], part_outs[at], sems.at[at]))
    for store in stores:
        store.start()
    half = rows // 2
    dq_outs[0][...] = dq_ref[0] + own_q_ref[...]
    for at in range(1, ring // 2):
        dq_outs[at][...] = dq_ref[at].astype(BF16)
        dq_outs[ring // 2 + at][...] = dq_ref[ring // 2 + at].astype(BF16)
    dq_outs[ring // 2][...] = dq_ref[ring // 2, :half].astype(BF16)
    dq_outs[ring][...] = dq_ref[ring // 2, half:].astype(BF16)
    for at in range(PAIR, owners):
        far_ref[at - PAIR] = acc_ref[at].astype(BF16)
        turned = pltpu.make_async_copy(far_ref.at[at - PAIR], part_outs[at], sems.at[at])
        turned.start()
        stores.append(turned)
    for store in stores:
        store.wait()


def slot_codes(table, j, p, x, owners):
    ring, blocks, heads, top_count = table.shape
    slot_total = ring * owners * PER_PEER
    span = blocks * owners
    flat = table.reshape(-1)
    ids = jnp.arange(flat.shape[0], dtype=jnp.int32)
    hit = (flat >= 0) & (flat // span == j)
    owner = flat % span // blocks
    near = (owner % X_SIZE - x) % X_SIZE * PAIR + (owner // X_SIZE - p) % PAIR
    code = ids // top_count * span + near * blocks + flat % blocks
    earlier = (ids[None, :] <= ids[:, None]) & hit[None, :]
    place = jnp.sum(earlier.astype(jnp.int32), axis=1) - 1
    match = (place[None, :] == jnp.arange(slot_total, dtype=jnp.int32)[:, None]) & hit[None, :]
    codes = jnp.sum(jnp.where(match, code[None, :], 0), axis=1)
    return jnp.concatenate([jnp.sum(hit.astype(jnp.int32))[None], codes, j[None]])


def remote_call(codes, stats, own_q, packs, own_k, own_v, kvs, blocks, heads, factor, rows, width, ring, owners):
    anywhere = pl.BlockSpec(memory_space=pl.ANY)
    part = (2 * rows, width)
    return pl.pallas_call(
        functools.partial(remote_kernel, blocks, heads, factor, owners),
        in_specs=[pl.BlockSpec(memory_space=pltpu.SMEM)]
        + [pl.BlockSpec(memory_space=pltpu.VMEM)] * 4
        + [anywhere] * (1 + owners),
        out_specs=(pl.BlockSpec(memory_space=pltpu.VMEM),) * (ring + 1) + (anywhere,) * owners,
        out_shape=(jax.ShapeDtypeStruct((rows, width), F32),)
        + (jax.ShapeDtypeStruct((rows, width), BF16),) * (ring // 2 - 1)
        + (jax.ShapeDtypeStruct((rows // 2, width), BF16),)
        + (jax.ShapeDtypeStruct((rows, width), BF16),) * (ring // 2 - 1)
        + (jax.ShapeDtypeStruct((rows // 2, width), BF16),)
        + (jax.ShapeDtypeStruct(part, F32),) * PAIR
        + (jax.ShapeDtypeStruct(part, BF16),) * (owners - PAIR),
        scratch_shapes=[
            pltpu.VMEM((ring, rows, width), F32),
            pltpu.VMEM((owners, *part), F32),
            pltpu.VMEM((owners - PAIR, *part), BF16),
            pltpu.VMEM((BLOCK, BLOCK), F32),
            pltpu.VMEM((ring, 2 * rows, width), BF16),
            pltpu.VMEM((owners, *part), BF16),
            pltpu.SemaphoreType.DMA((owners + 1,)),
        ],
        compiler_params=PARAMS,
        name="remote",
    )(codes, stats, own_q, own_k, own_v, packs, *kvs)


def shards(queries, keys, values, out_grad, outputs, log_norms, selected):
    blocks, heads, top_count = selected.shape
    rows, width = queries.shape
    factor = (width // heads) ** (-0.5)
    ring = lax.axis_size("j")
    owners = lax.axis_size("p") * lax.axis_size("x")
    pack = pl.pallas_call(
        pack_kernel,
        out_shape=jax.ShapeDtypeStruct((2 * rows, width), BF16),
        compiler_params=PARAMS,
        name="pack",
    )(queries, out_grad)
    packs = lax.all_gather(pack, "j")
    pack, selected, keys, values = lax.optimization_barrier((pack, selected, keys, values))
    both = jnp.concatenate([keys, values], axis=0)
    swapped = lax.ppermute(both, "p", [(i, (i + 1) % PAIR) for i in range(PAIR)])
    kvs = [both, swapped]
    for shift in range(1, X_SIZE):
        back = [(i, (i - shift) % X_SIZE) for i in range(X_SIZE)]
        kvs += [lax.ppermute(both, "x", back), lax.ppermute(swapped, "x", back)]
    own = jax.ShapeDtypeStruct((rows, width), F32)
    stats, own_q, own_k, own_v = pl.pallas_call(
        functools.partial(own_kernel, blocks, heads, factor),
        out_shape=(jax.ShapeDtypeStruct((2 * blocks * heads, BLOCK), F32), own, own, own),
        compiler_params=PARAMS,
        name="own",
    )(queries, out_grad, outputs, log_norms.T, keys, values)
    stats, selected, swapped = lax.optimization_barrier((stats, selected, swapped))
    picks = jnp.pad(selected.reshape(-1).astype(F32), (0, BLOCK * 8 - selected.size))
    info = jnp.concatenate([stats, picks.reshape(8, BLOCK)], axis=0)
    stats = lax.all_to_all(jnp.broadcast_to(info[None], (ring, *info.shape)), "j", 0, 0, tiled=True)
    table = stats[:, 2 * blocks * heads, : selected.size].astype(jnp.int32)
    table = table.reshape(ring, *selected.shape)
    codes = slot_codes(table, lax.axis_index("j"), lax.axis_index("p"), lax.axis_index("x"), owners)
    packs, kvs, codes, stats, own_q, own_k, own_v = lax.optimization_barrier(
        (packs, kvs, codes, stats, own_q, own_k, own_v)
    )
    outs = remote_call(
        codes, stats, own_q, packs, own_k, own_v, kvs, blocks, heads, factor, rows, width, ring, owners
    )
    near_q, *far_q = outs[: ring + 1]
    near, near_other, next_a, next_b, far_a, far_b, last_a, last_b = outs[ring + 1 :]
    ahead = [(i, (i + 1) % X_SIZE) for i in range(X_SIZE)]
    behind = [(i, (i - 1) % X_SIZE) for i in range(X_SIZE)]

    def wide(part):
        return part.astype(F32)

    up = [(i, (i + 1) % ring) for i in range(ring)]
    down = [(i, (i - 1) % ring) for i in range(ring)]
    middle, half = ring // 2, rows // 2
    rising = lax.ppermute(far_q[middle - 1], "j", up)
    falling = lax.ppermute(far_q[ring - 1], "j", down)
    part = far_q[middle - 2]
    rising = jnp.concatenate([(wide(part[:half]) + wide(rising)).astype(BF16), part[half:]])
    part = far_q[middle]
    falling = jnp.concatenate([part[:half], (wide(part[half:]) + wide(falling)).astype(BF16)])
    for step in range(1, middle - 1):
        rising = lax.ppermute(rising, "j", up)
        falling = lax.ppermute(falling, "j", down)
        rising = (wide(far_q[middle - 2 - step]) + wide(rising)).astype(BF16)
        falling = (wide(far_q[middle + step]) + wide(falling)).astype(BF16)
    rising = lax.ppermute(rising, "j", up)
    falling = lax.ppermute(falling, "j", down)
    sum_q = (near_q + wide(rising) + wide(falling)).astype(BF16)

    through_a = lax.ppermute(far_a, "x", ahead)
    through_b = lax.ppermute(far_b, "x", behind)
    from_next = lax.ppermute(next_b, "x", ahead)
    from_last = lax.ppermute(last_a, "x", behind)
    next_a = (wide(next_a) + wide(through_a)).astype(BF16)
    last_b = (wide(last_b) + wide(through_b)).astype(BF16)
    sum_own = near + wide(from_last) + wide(lax.ppermute(next_a, "x", ahead))
    sum_other = near_other + wide(from_next) + wide(lax.ppermute(last_b, "x", behind))
    sum_other, sum_own, sum_q = lax.optimization_barrier((sum_other.astype(BF16), sum_own, sum_q))
    crossed = lax.ppermute(sum_other, "p", [(i, (i + 1) % PAIR) for i in range(PAIR)])
    final_kv = sum_own + wide(crossed)
    final_k = final_kv[:rows].astype(BF16)
    final_v = final_kv[rows:].astype(BF16)
    spread_q = lax.all_to_all(sum_q, "head", split_axis=0, concat_axis=1, tiled=True)
    return spread_q, final_k, final_v


def solution(mesh):
    ctx_count, head_count = mesh.devices.shape
    grid = mesh.devices.reshape(ctx_count // (PAIR * X_SIZE), PAIR, X_SIZE, head_count)
    fine = Mesh(grid, ("j", "p", "x", "head"))
    ctx = ("j", "p", "x")
    placed = P(ctx, "head")
    return jax.shard_map(
        shards,
        mesh=fine,
        in_specs=(placed,) * 6 + (P(ctx, "head", None),),
        out_specs=(P((*ctx, "head"), None), placed, placed),
        check_vma=False,
    )
```

```python
import functools

import jax
import jax.numpy as jnp
from jax import lax
from jax.experimental import pallas as pl
from jax.experimental.pallas import tpu as pltpu
from jax.sharding import Mesh
from jax.sharding import PartitionSpec as P

X_SIZE = 4
BLOCK = 128
PER_PEER = 2
PAIR = 2
TURN_SIZES = (16, 4)
F32 = jnp.float32
BF16 = jnp.bfloat16
PARAMS = pltpu.CompilerParams(vmem_limit_bytes=56 * 1024 * 1024)


def mm(left, right, left_dim, right_dim):
    return lax.dot_general(
        left, right, (((left_dim,), (right_dim,)), ((), ())), preferred_element_type=F32
    )


def pack_kernel(q_ref, g_ref, out_ref):
    rows = q_ref.shape[0]
    out_ref[:rows] = q_ref[...]
    out_ref[rows:] = g_ref[...]


def stat_row(b, h, heads):
    return 2 * (b * heads + h)


def pair_terms(q, g, k, v, norm, delta, factor, keep):
    blank = jnp.zeros_like(q)
    queries = jnp.concatenate(
        [jnp.concatenate([q, blank], axis=1), jnp.concatenate([blank, g], axis=1)], axis=0
    )
    products = mm(jnp.concatenate([k, v], axis=1), queries, 1, 1)
    scores = products[:, :BLOCK] * factor
    weights = jnp.where(keep, jnp.exp(scores - norm), 0.0)
    dscores = weights * (products[:, BLOCK:] - delta)
    weights_b = weights.astype(BF16)
    dscores_b = dscores.astype(BF16)
    grads = mm(jnp.concatenate([dscores_b, weights_b], axis=1), queries, 1, 0)
    grad_q = mm(dscores_b, k, 0, 0) * factor
    return grad_q, grads[:, :BLOCK] * factor, grads[:, BLOCK:]


def own_kernel(
    blocks, heads, factor, q_ref, g_ref, o_ref, n_ref, k_ref, v_ref, stat_ref, dq_ref, dk_ref, dv_ref
):
    key_at = lax.broadcasted_iota(jnp.int32, (BLOCK, BLOCK), 0)
    query_at = lax.broadcasted_iota(jnp.int32, (BLOCK, BLOCK), 1)
    keep = key_at <= query_at
    for b in range(blocks):
        for h in range(heads):
            at = slice(b * BLOCK, (b + 1) * BLOCK)
            cols = slice(h * BLOCK, (h + 1) * BLOCK)
            product = g_ref[at, cols].astype(F32) * o_ref[at, cols].astype(F32)
            delta = jnp.sum(product.T, axis=0, keepdims=True)
            norm = n_ref[h : h + 1, at]
            row = stat_row(b, h, heads)
            stat_ref[row : row + 1] = norm
            stat_ref[row + 1 : row + 2] = delta
            grad_q, grad_k, grad_v = pair_terms(
                q_ref[at, cols], g_ref[at, cols], k_ref[at, cols], v_ref[at, cols], norm, delta, factor, keep
            )
            dq_ref[at, cols] = grad_q
            dk_ref[at, cols] = grad_k
            dv_ref[at, cols] = grad_v


def low_bits(value, size):
    return value & (size - 1), value >> (size.bit_length() - 1)


def remote_kernel(blocks, heads, factor, owners, *refs):
    slots_ref, stat_ref, own_q_ref, own_k_ref, own_v_ref, packs_ref = refs[:6]
    kv_refs = refs[6 : 6 + owners]
    dq_out, *part_outs = refs[6 + owners : 7 + 2 * owners]
    dq_ref, acc_ref, far_ref, line_ref, pack_ref, kv_ref, sems = refs[7 + 2 * owners :]
    rows = blocks * BLOCK
    span = blocks * owners
    loads = [
        pltpu.make_async_copy(packs_ref, pack_ref, sems.at[owners]),
    ]
    for at in range(owners):
        loads.append(pltpu.make_async_copy(kv_refs[at], kv_ref.at[at], sems.at[at]))
    for load in loads:
        load.start()
    count = slots_ref[0]
    mine = slots_ref[slots_ref.shape[0] - 1]
    dq_ref[...] = jnp.zeros_like(dq_ref)
    dq_ref[mine] = own_q_ref[...].astype(BF16)
    acc_ref[0, :rows] = own_k_ref[...]
    acc_ref[0, rows:] = own_v_ref[...]
    acc_ref[1:] = jnp.zeros((owners - 1, *acc_ref.shape[1:]), F32)
    for load in loads:
        load.wait()

    def turn(first, size):
        done = []
        for u in range(size):
            slot = first + u
            live = slot < count
            code = slots_ref[1 + jnp.where(live, slot, count - 1)]
            kb, rest = low_bits(code, blocks)
            kx, rest = low_bits(rest, owners)
            h, rest = low_bits(rest, heads)
            b, zq = low_bits(rest, blocks)
            cols = pl.ds(pl.multiple_of(h * BLOCK, BLOCK), BLOCK)
            q_at = pl.ds(pl.multiple_of(b * BLOCK, BLOCK), BLOCK)
            g_at = pl.ds(pl.multiple_of(rows + b * BLOCK, BLOCK), BLOCK)
            k_at = pl.ds(pl.multiple_of(kb * BLOCK, BLOCK), BLOCK)
            v_at = pl.ds(pl.multiple_of(rows + kb * BLOCK, BLOCK), BLOCK)
            row = stat_row(b, h, heads)
            norm = stat_ref[zq, pl.ds(row, 1), :]
            delta = stat_ref[zq, pl.ds(row + 1, 1), :]
            terms = pair_terms(
                pack_ref[zq, q_at, cols],
                pack_ref[zq, g_at, cols],
                kv_ref[kx, k_at, cols],
                kv_ref[kx, v_at, cols],
                norm,
                delta,
                factor,
                live,
            )
            before = slots_ref[jnp.where(live, slot, count)]
            shift = span.bit_length() - 1
            same = (slot > 0) & ((before >> shift) == (code >> shift))
            done.append((same, zq, q_at, cols, kx, k_at, v_at, terms))
        for same, zq, q_at, cols, kx, k_at, v_at, (grad_q, grad_k, grad_v) in done:
            acc_ref[kx, k_at, cols] += grad_k
            acc_ref[kx, v_at, cols] += grad_v
            start = jnp.where(zq == mine, own_q_ref[q_at, cols], 0.0)
            total = jnp.where(same, line_ref[...], start) + grad_q
            line_ref[...] = total
            dq_ref[zq, q_at, cols] = total.astype(BF16)

    large, small = TURN_SIZES
    full, rest = low_bits(count, large)[::-1]

    @pl.loop(0, full)
    def _(step):
        turn(step * large, large)

    @pl.loop(0, low_bits(rest + small - 1, small)[1])
    def _(step):
        turn(full * large + step * small, small)

    stores = [pltpu.make_async_copy(dq_ref, dq_out, sems.at[owners])]
    for at in range(PAIR):
        stores.append(pltpu.make_async_copy(acc_ref.at[at], part_outs[at], sems.at[at]))
    for store in stores:
        store.start()
    for at in range(PAIR, owners):
        far_ref[at - PAIR] = acc_ref[at].astype(BF16)
        turned = pltpu.make_async_copy(far_ref.at[at - PAIR], part_outs[at], sems.at[at])
        turned.start()
        stores.append(turned)
    for store in stores:
        store.wait()


def slot_codes(table, j, p, x, owners):
    ring, blocks, heads, top_count = table.shape
    slot_total = ring * owners * PER_PEER
    span = blocks * owners
    flat = table.reshape(-1)
    ids = jnp.arange(flat.shape[0], dtype=jnp.int32)
    hit = (flat >= 0) & (flat // span == j)
    owner = flat % span // blocks
    near = (owner % X_SIZE - x) % X_SIZE * PAIR + (owner // X_SIZE - p) % PAIR
    code = ids // top_count * span + near * blocks + flat % blocks
    earlier = (ids[None, :] <= ids[:, None]) & hit[None, :]
    place = jnp.sum(earlier.astype(jnp.int32), axis=1) - 1
    match = (place[None, :] == jnp.arange(slot_total, dtype=jnp.int32)[:, None]) & hit[None, :]
    codes = jnp.sum(jnp.where(match, code[None, :], 0), axis=1)
    return jnp.concatenate([jnp.sum(hit.astype(jnp.int32))[None], codes, j[None]])


def remote_call(codes, stats, own_q, packs, own_k, own_v, kvs, blocks, heads, factor, rows, width, ring, owners):
    anywhere = pl.BlockSpec(memory_space=pl.ANY)
    part = (2 * rows, width)
    return pl.pallas_call(
        functools.partial(remote_kernel, blocks, heads, factor, owners),
        in_specs=[pl.BlockSpec(memory_space=pltpu.SMEM)]
        + [pl.BlockSpec(memory_space=pltpu.VMEM)] * 4
        + [anywhere] * (1 + owners),
        out_specs=(anywhere,) * (1 + owners),
        out_shape=(jax.ShapeDtypeStruct((ring, rows, width), BF16),)
        + (jax.ShapeDtypeStruct(part, F32),) * PAIR
        + (jax.ShapeDtypeStruct(part, BF16),) * (owners - PAIR),
        scratch_shapes=[
            pltpu.VMEM((ring, rows, width), BF16),
            pltpu.VMEM((owners, *part), F32),
            pltpu.VMEM((owners - PAIR, *part), BF16),
            pltpu.VMEM((BLOCK, BLOCK), F32),
            pltpu.VMEM((ring, 2 * rows, width), BF16),
            pltpu.VMEM((owners, *part), BF16),
            pltpu.SemaphoreType.DMA((owners + 1,)),
        ],
        compiler_params=PARAMS,
        name="remote",
    )(codes, stats, own_q, own_k, own_v, packs, *kvs)


def shards(queries, keys, values, out_grad, outputs, log_norms, selected):
    blocks, heads, top_count = selected.shape
    rows, width = queries.shape
    factor = (width // heads) ** (-0.5)
    ring = lax.axis_size("j")
    owners = lax.axis_size("p") * lax.axis_size("x")
    pack = pl.pallas_call(
        pack_kernel,
        out_shape=jax.ShapeDtypeStruct((2 * rows, width), BF16),
        compiler_params=PARAMS,
        name="pack",
    )(queries, out_grad)
    packs = lax.all_gather(pack, "j")
    pack, selected, keys, values = lax.optimization_barrier((pack, selected, keys, values))
    cross = [(i, (i + 1) % PAIR) for i in range(PAIR)]
    swapped = jnp.concatenate([lax.ppermute(keys, "p", cross), lax.ppermute(values, "p", cross)], axis=0)
    both = jnp.concatenate([keys, values], axis=0)
    kvs = [both, swapped]
    for shift in range(1, X_SIZE):
        back = [(i, (i - shift) % X_SIZE) for i in range(X_SIZE)]
        kvs += [lax.ppermute(both, "x", back), lax.ppermute(swapped, "x", back)]
    own = jax.ShapeDtypeStruct((rows, width), F32)
    stats, own_q, own_k, own_v = pl.pallas_call(
        functools.partial(own_kernel, blocks, heads, factor),
        out_shape=(jax.ShapeDtypeStruct((2 * blocks * heads, BLOCK), F32), own, own, own),
        compiler_params=PARAMS,
        name="own",
    )(queries, out_grad, outputs, log_norms.T, keys, values)
    stats, selected, swapped = lax.optimization_barrier((stats, selected, swapped))
    picks = jnp.pad(selected.reshape(-1).astype(F32), (0, BLOCK * 8 - selected.size))
    info = jnp.concatenate([stats, picks.reshape(8, BLOCK)], axis=0)
    stats = lax.all_to_all(jnp.broadcast_to(info[None], (ring, *info.shape)), "j", 0, 0, tiled=True)
    table = stats[:, 2 * blocks * heads, : selected.size].astype(jnp.int32)
    table = table.reshape(ring, *selected.shape)
    codes = slot_codes(table, lax.axis_index("j"), lax.axis_index("p"), lax.axis_index("x"), owners)
    packs, kvs, codes, stats, own_q, own_k, own_v = lax.optimization_barrier(
        (packs, kvs, codes, stats, own_q, own_k, own_v)
    )
    part_q, near, near_other, next_a, next_b, far_a, far_b, last_a, last_b = remote_call(
        codes, stats, own_q, packs, own_k, own_v, kvs, blocks, heads, factor, rows, width, ring, owners
    )
    sum_q = lax.psum_scatter(part_q, "j", scatter_dimension=0)
    ahead = [(i, (i + 1) % X_SIZE) for i in range(X_SIZE)]
    behind = [(i, (i - 1) % X_SIZE) for i in range(X_SIZE)]

    def wide(part):
        return part.astype(F32)

    through_a = lax.ppermute(far_a, "x", ahead)
    through_b = lax.ppermute(far_b, "x", behind)
    from_next = lax.ppermute(next_b, "x", ahead)
    from_last = lax.ppermute(last_a, "x", behind)
    next_a = (wide(next_a) + wide(through_a)).astype(BF16)
    last_b = (wide(last_b) + wide(through_b)).astype(BF16)
    sum_own = near + wide(from_last) + wide(lax.ppermute(next_a, "x", ahead))
    sum_other = near_other + wide(from_next) + wide(lax.ppermute(last_b, "x", behind))
    sum_other, sum_own, sum_q = lax.optimization_barrier((sum_other.astype(BF16), sum_own, sum_q))
    crossed = lax.ppermute(sum_other, "p", [(i, (i + 1) % PAIR) for i in range(PAIR)])
    final_kv = sum_own + wide(crossed)
    final_k = final_kv[:rows].astype(BF16)
    final_v = final_kv[rows:].astype(BF16)
    spread_q = lax.all_to_all(sum_q, "head", split_axis=0, concat_axis=1, tiled=True)
    return spread_q, final_k, final_v


def solution(mesh):
    ctx_count, head_count = mesh.devices.shape
    grid = mesh.devices.reshape(ctx_count // (PAIR * X_SIZE), PAIR, X_SIZE, head_count)
    fine = Mesh(grid, ("j", "p", "x", "head"))
    ctx = ("j", "p", "x")
    placed = P(ctx, "head")
    return jax.shard_map(
        shards,
        mesh=fine,
        in_specs=(placed,) * 6 + (P(ctx, "head", None),),
        out_specs=(P((*ctx, "head"), None), placed, placed),
        check_vma=False,
    )
```

```python
import functools

import jax
import jax.numpy as jnp
from jax import lax
from jax.experimental import pallas as pl
from jax.experimental.pallas import tpu as pltpu
from jax.sharding import Mesh
from jax.sharding import PartitionSpec as P

X_SIZE = 4
BLOCK = 128
PER_PEER = 2
PAIR = 2
TURN_SIZES = (16, 4)
F32 = jnp.float32
BF16 = jnp.bfloat16
LARGEST = float(jnp.finfo(jnp.bfloat16).max)
PARAMS = pltpu.CompilerParams(vmem_limit_bytes=56 * 1024 * 1024)


def mm(left, right, left_dim, right_dim):
    return lax.dot_general(
        left, right, (((left_dim,), (right_dim,)), ((), ())), preferred_element_type=F32
    )


def pack_kernel(q_ref, g_ref, out_ref):
    rows = q_ref.shape[0]
    out_ref[:rows] = q_ref[...]
    out_ref[rows:] = g_ref[...]


def stat_row(b, h, heads):
    return 2 * (b * heads + h)


def pair_terms(q, g, k, v, norm, delta, factor, keep):
    blank = jnp.zeros_like(q)
    queries = jnp.concatenate(
        [jnp.concatenate([q, blank], axis=1), jnp.concatenate([blank, g], axis=1)], axis=0
    )
    products = mm(jnp.concatenate([k, v], axis=1), queries, 1, 1)
    scores = products[:, :BLOCK] * factor
    weights = jnp.where(keep, jnp.exp(scores - norm), 0.0)
    dscores = weights * (products[:, BLOCK:] - delta)
    dscores = jnp.clip(dscores, -LARGEST, LARGEST)
    weights_b = weights.astype(BF16)
    dscores_b = dscores.astype(BF16)
    grads = mm(jnp.concatenate([dscores_b, weights_b], axis=1), queries, 1, 0)
    grad_q = mm(dscores_b, k, 0, 0) * factor
    return grad_q, grads[:, :BLOCK] * factor, grads[:, BLOCK:]


def own_kernel(
    blocks, heads, factor, q_ref, g_ref, o_ref, n_ref, k_ref, v_ref, stat_ref, dq_ref, dk_ref, dv_ref
):
    key_at = lax.broadcasted_iota(jnp.int32, (BLOCK, BLOCK), 0)
    query_at = lax.broadcasted_iota(jnp.int32, (BLOCK, BLOCK), 1)
    keep = key_at <= query_at
    for b in range(blocks):
        for h in range(heads):
            at = slice(b * BLOCK, (b + 1) * BLOCK)
            cols = slice(h * BLOCK, (h + 1) * BLOCK)
            product = g_ref[at, cols].astype(F32) * o_ref[at, cols].astype(F32)
            delta = jnp.sum(product.T, axis=0, keepdims=True)
            norm = n_ref[h : h + 1, at]
            row = stat_row(b, h, heads)
            stat_ref[row : row + 1] = norm
            stat_ref[row + 1 : row + 2] = delta
            grad_q, grad_k, grad_v = pair_terms(
                q_ref[at, cols], g_ref[at, cols], k_ref[at, cols], v_ref[at, cols], norm, delta, factor, keep
            )
            dq_ref[at, cols] = grad_q
            dk_ref[at, cols] = grad_k
            dv_ref[at, cols] = grad_v


def low_bits(value, size):
    return value & (size - 1), value >> (size.bit_length() - 1)


def remote_kernel(blocks, heads, factor, owners, *refs):
    slots_ref, stat_ref, own_q_ref, own_k_ref, own_v_ref, packs_ref = refs[:6]
    kv_refs = refs[6 : 6 + owners]
    dq_out, *part_outs = refs[6 + owners : 7 + 2 * owners]
    dq_ref, acc_ref, far_ref, line_ref, pack_ref, kv_ref, sems = refs[7 + 2 * owners :]
    rows = blocks * BLOCK
    span = blocks * owners
    loads = [
        pltpu.make_async_copy(packs_ref, pack_ref, sems.at[owners]),
    ]
    for at in range(owners):
        loads.append(pltpu.make_async_copy(kv_refs[at], kv_ref.at[at], sems.at[at]))
    for load in loads:
        load.start()
    count = slots_ref[0]
    mine = slots_ref[slots_ref.shape[0] - 1]
    dq_ref[...] = jnp.zeros_like(dq_ref)
    dq_ref[mine] = own_q_ref[...].astype(BF16)
    acc_ref[0, :rows] = own_k_ref[...]
    acc_ref[0, rows:] = own_v_ref[...]
    acc_ref[1:] = jnp.zeros((owners - 1, *acc_ref.shape[1:]), F32)
    for load in loads:
        load.wait()

    def turn(first, size):
        done = []
        for u in range(size):
            slot = first + u
            live = slot < count
            code = slots_ref[1 + jnp.where(live, slot, count - 1)]
            kb, rest = low_bits(code, blocks)
            kx, rest = low_bits(rest, owners)
            h, rest = low_bits(rest, heads)
            b, zq = low_bits(rest, blocks)
            cols = pl.ds(pl.multiple_of(h * BLOCK, BLOCK), BLOCK)
            q_at = pl.ds(pl.multiple_of(b * BLOCK, BLOCK), BLOCK)
            g_at = pl.ds(pl.multiple_of(rows + b * BLOCK, BLOCK), BLOCK)
            k_at = pl.ds(pl.multiple_of(kb * BLOCK, BLOCK), BLOCK)
            v_at = pl.ds(pl.multiple_of(rows + kb * BLOCK, BLOCK), BLOCK)
            row = stat_row(b, h, heads)
            norm = stat_ref[zq, pl.ds(row, 1), :]
            delta = stat_ref[zq, pl.ds(row + 1, 1), :]
            terms = pair_terms(
                pack_ref[zq, q_at, cols],
                pack_ref[zq, g_at, cols],
                kv_ref[kx, k_at, cols],
                kv_ref[kx, v_at, cols],
                norm,
                delta,
                factor,
                live,
            )
            before = slots_ref[jnp.where(live, slot, count)]
            shift = span.bit_length() - 1
            same = (slot > 0) & ((before >> shift) == (code >> shift))
            done.append((same, zq, q_at, cols, kx, k_at, v_at, terms))
        for same, zq, q_at, cols, kx, k_at, v_at, (grad_q, grad_k, grad_v) in done:
            acc_ref[kx, k_at, cols] += grad_k
            acc_ref[kx, v_at, cols] += grad_v
            start = jnp.where(zq == mine, own_q_ref[q_at, cols], 0.0)
            total = jnp.where(same, line_ref[...], start) + grad_q
            line_ref[...] = total
            dq_ref[zq, q_at, cols] = total.astype(BF16)

    large, small = TURN_SIZES
    full, rest = low_bits(count, large)[::-1]

    @pl.loop(0, full)
    def _(step):
        turn(step * large, large)

    @pl.loop(0, low_bits(rest + small - 1, small)[1])
    def _(step):
        turn(full * large + step * small, small)

    stores = [pltpu.make_async_copy(dq_ref, dq_out, sems.at[owners])]
    for at in range(PAIR):
        stores.append(pltpu.make_async_copy(acc_ref.at[at], part_outs[at], sems.at[at]))
    for store in stores:
        store.start()
    for at in range(PAIR, owners):
        far_ref[at - PAIR] = acc_ref[at].astype(BF16)
        turned = pltpu.make_async_copy(far_ref.at[at - PAIR], part_outs[at], sems.at[at])
        turned.start()
        stores.append(turned)
    for store in stores:
        store.wait()


def slot_codes(table, j, p, x, owners):
    ring, blocks, heads, top_count = table.shape
    slot_total = ring * owners * PER_PEER
    span = blocks * owners
    flat = table.reshape(-1)
    ids = jnp.arange(flat.shape[0], dtype=jnp.int32)
    hit = (flat >= 0) & (flat // span == j)
    owner = flat % span // blocks
    near = (owner % X_SIZE - x) % X_SIZE * PAIR + (owner // X_SIZE - p) % PAIR
    code = ids // top_count * span + near * blocks + flat % blocks
    earlier = (ids[None, :] <= ids[:, None]) & hit[None, :]
    place = jnp.sum(earlier.astype(jnp.int32), axis=1) - 1
    match = (place[None, :] == jnp.arange(slot_total, dtype=jnp.int32)[:, None]) & hit[None, :]
    codes = jnp.sum(jnp.where(match, code[None, :], 0), axis=1)
    return jnp.concatenate([jnp.sum(hit.astype(jnp.int32))[None], codes, j[None]])


def remote_call(codes, stats, own_q, packs, own_k, own_v, kvs, blocks, heads, factor, rows, width, ring, owners):
    anywhere = pl.BlockSpec(memory_space=pl.ANY)
    part = (2 * rows, width)
    return pl.pallas_call(
        functools.partial(remote_kernel, blocks, heads, factor, owners),
        in_specs=[pl.BlockSpec(memory_space=pltpu.SMEM)]
        + [pl.BlockSpec(memory_space=pltpu.VMEM)] * 4
        + [anywhere] * (1 + owners),
        out_specs=(anywhere,) * (1 + owners),
        out_shape=(jax.ShapeDtypeStruct((ring, rows, width), BF16),)
        + (jax.ShapeDtypeStruct(part, F32),) * PAIR
        + (jax.ShapeDtypeStruct(part, BF16),) * (owners - PAIR),
        scratch_shapes=[
            pltpu.VMEM((ring, rows, width), BF16),
            pltpu.VMEM((owners, *part), F32),
            pltpu.VMEM((owners - PAIR, *part), BF16),
            pltpu.VMEM((BLOCK, BLOCK), F32),
            pltpu.VMEM((ring, 2 * rows, width), BF16),
            pltpu.VMEM((owners, *part), BF16),
            pltpu.SemaphoreType.DMA((owners + 1,)),
        ],
        compiler_params=PARAMS,
        name="remote",
    )(codes, stats, own_q, own_k, own_v, packs, *kvs)


def shards(queries, keys, values, out_grad, outputs, log_norms, selected):
    blocks, heads, top_count = selected.shape
    rows, width = queries.shape
    factor = (width // heads) ** (-0.5)
    ring = lax.axis_size("j")
    owners = lax.axis_size("p") * lax.axis_size("x")
    pack = pl.pallas_call(
        pack_kernel,
        out_shape=jax.ShapeDtypeStruct((2 * rows, width), BF16),
        compiler_params=PARAMS,
        name="pack",
    )(queries, out_grad)
    packs = lax.all_gather(pack, "j")
    pack, selected, keys, values = lax.optimization_barrier((pack, selected, keys, values))
    both = jnp.concatenate([keys, values], axis=0)
    swapped = lax.ppermute(both, "p", [(i, (i + 1) % PAIR) for i in range(PAIR)])
    kvs = [both, swapped]
    for shift in range(1, X_SIZE):
        back = [(i, (i - shift) % X_SIZE) for i in range(X_SIZE)]
        kvs += [lax.ppermute(both, "x", back), lax.ppermute(swapped, "x", back)]
    own = jax.ShapeDtypeStruct((rows, width), F32)
    stats, own_q, own_k, own_v = pl.pallas_call(
        functools.partial(own_kernel, blocks, heads, factor),
        out_shape=(jax.ShapeDtypeStruct((2 * blocks * heads, BLOCK), F32), own, own, own),
        compiler_params=PARAMS,
        name="own",
    )(queries, out_grad, outputs, log_norms.T, keys, values)
    stats, selected, swapped = lax.optimization_barrier((stats, selected, swapped))
    picks = jnp.pad(selected.reshape(-1).astype(F32), (0, BLOCK * 8 - selected.size))
    info = jnp.concatenate([stats, picks.reshape(8, BLOCK)], axis=0)
    stats = lax.all_to_all(jnp.broadcast_to(info[None], (ring, *info.shape)), "j", 0, 0, tiled=True)
    table = stats[:, 2 * blocks * heads, : selected.size].astype(jnp.int32)
    table = table.reshape(ring, *selected.shape)
    codes = slot_codes(table, lax.axis_index("j"), lax.axis_index("p"), lax.axis_index("x"), owners)
    packs, kvs, codes, stats, own_q, own_k, own_v = lax.optimization_barrier(
        (packs, kvs, codes, stats, own_q, own_k, own_v)
    )
    part_q, near, near_other, next_a, next_b, far_a, far_b, last_a, last_b = remote_call(
        codes, stats, own_q, packs, own_k, own_v, kvs, blocks, heads, factor, rows, width, ring, owners
    )
    sum_q = lax.psum_scatter(part_q, "j", scatter_dimension=0)
    ahead = [(i, (i + 1) % X_SIZE) for i in range(X_SIZE)]
    behind = [(i, (i - 1) % X_SIZE) for i in range(X_SIZE)]

    def wide(part):
        return part.astype(F32)

    through_a = lax.ppermute(far_a, "x", ahead)
    through_b = lax.ppermute(far_b, "x", behind)
    from_next = lax.ppermute(next_b, "x", ahead)
    from_last = lax.ppermute(last_a, "x", behind)
    next_a = (wide(next_a) + wide(through_a)).astype(BF16)
    last_b = (wide(last_b) + wide(through_b)).astype(BF16)
    sum_own = near + wide(from_last) + wide(lax.ppermute(next_a, "x", ahead))
    sum_other = near_other + wide(from_next) + wide(lax.ppermute(last_b, "x", behind))
    sum_other, sum_own, sum_q = lax.optimization_barrier((sum_other.astype(BF16), sum_own, sum_q))
    crossed = lax.ppermute(sum_other, "p", [(i, (i + 1) % PAIR) for i in range(PAIR)])
    final_kv = sum_own + wide(crossed)
    final_k = final_kv[:rows].astype(BF16)
    final_v = final_kv[rows:].astype(BF16)
    spread_q = lax.all_to_all(sum_q, "head", split_axis=0, concat_axis=1, tiled=True)
    return spread_q, final_k, final_v


def solution(mesh):
    ctx_count, head_count = mesh.devices.shape
    grid = mesh.devices.reshape(ctx_count // (PAIR * X_SIZE), PAIR, X_SIZE, head_count)
    fine = Mesh(grid, ("j", "p", "x", "head"))
    ctx = ("j", "p", "x")
    placed = P(ctx, "head")
    return jax.shard_map(
        shards,
        mesh=fine,
        in_specs=(placed,) * 6 + (P(ctx, "head", None),),
        out_specs=(P((*ctx, "head"), None), placed, placed),
        check_vma=False,
    )
```
